32 devices in a mesh: group: 2 (over y), dom: 4 (over z), row: 4 (over x, core).
Axes of the slice: x: 2, y: 2, z: 4, core: 2. Of those that a mesh axis runs over, the one named last changes fastest.
Arguments:
- state: bfloat16 [8, 16, 10752], P(('group', 'dom'), 'row'), parts along dimension 0, may hold values from -6 to 6
- prev_pred: bfloat16 [8, 16, 10752], P(('group', 'dom'), 'row'), parts along dimension 0, may hold values from -6 to 6
- ancestors: int32 [8], P('group'), parts along dimension 0, may hold values from 0 to 3, as said below
- timestep: int32 [2], P('group'), parts along dimension 0, may hold values from 50 to 949
- w_in: bfloat16 [168, 256], replicated, may hold values from -0.5 to 0.5
- w_time: bfloat16 [256, 256], replicated, may hold values from -0.375 to 0.375
- w_qkv: bfloat16 [2, 256, 768], replicated, may hold values from -0.375 to 0.375
- w_attn_out: bfloat16 [2, 256, 256], replicated, may hold values from -0.375 to 0.375
- w_up: bfloat16 [2, 256, 1024], replicated, may hold values from -0.375 to 0.375
- w_down: bfloat16 [2, 1024, 256], replicated, may hold values from -0.1875 to 0.1875
- w_out: bfloat16 [256, 84], replicated, may hold values from -0.375 to 0.375
Outputs:
- new_state: bfloat16 [8, 16, 10752], P(('group', 'dom'), 'row'), parts along dimension 0
- new_pred: bfloat16 [8, 16, 10752], P(('group', 'dom'), 'row'), parts along dimension 0
The draws below stay inside these ranges and needn't reach their ends.
There are 2 independent parts, one for each index of `group`. The reference program is written for one: setup_inputs(seed, part) draws one part's arguments, and reference() takes and returns one part's arrays. A program takes and returns all parts, laid end to end along the dimension named above; an argument that names none is the same for every part. Nothing has to cross between parts.
Inputs may be any that keep to these rules, and one draw needn't show every extreme that they name: ancestors[j] is the particle of the same group whose state particle j takes; the list never falls.
All inputs are finite; a program needn't handle non-finite values.
Results may differ from the reference program's by a relative error of at most 0.018.
Values may be sent and summed in bfloat16 or wider, within the bound.
A program may use at most 64 MiB of HBM per device.

```python
import math
import jax
import jax.numpy as jnp
from jax import lax

D = 256
HEADS = 8
FF = 1024
CH = 84
COLS = 128
BLOCKS = 2
STEPS = 1000
STRIDE = 20
PARTICLES = 4
HEIGHT = 16


def draw_ancestors(key, part):
    base_key = jax.random.fold_in(key, 17)
    score_key, offset_key = jax.random.split(base_key)
    levels = jax.random.randint(score_key, (PARTICLES,), 0, 8)
    masses = jnp.left_shift(jnp.ones_like(levels), levels).astype(jnp.int32)
    totals = jnp.cumsum(masses).astype(jnp.int32)
    overall = totals[-1]
    offset = jax.random.randint(offset_key, (), 0, overall)
    points = jnp.arange(PARTICLES, dtype=jnp.int32) * overall + offset
    lineage = jnp.sum((totals[None, :] * PARTICLES <= points[:, None]).astype(jnp.int32), axis=1)
    return lineage.astype(jnp.int32)


def block_scale(key, extent, cuts, low, top_value):
    def one(position, shards_of):
        steps = jax.random.uniform(jax.random.fold_in(jax.random.fold_in(key, 6), position), (shards_of,), jnp.float32, low / len(cuts), top_value / len(cuts))
        return jnp.repeat(jnp.exp(steps), extent[position] // shards_of).reshape((-1,) + (1,) * (len(extent) - position - 1))

    gain = one(*cuts[0])
    for cut in cuts[1:]:
        gain = gain * one(*cut)
    return gain


def gaussian(key, extent, spread, bound, cuts=(), kind=jnp.bfloat16):
    gain = block_scale(key, extent, cuts, -0.22, 0.18) if cuts else 1.0
    values = jax.random.normal(key, extent, jnp.float32) * spread * gain
    return jnp.minimum(jnp.maximum(values, -bound), bound).astype(kind)


def setup_inputs(seed: int = 0, part: int = 0) -> dict:
    key_of = jax.random.split(jax.random.key(seed), 12)
    part_keys = jax.random.split(jax.random.fold_in(key_of[11], part), 12)
    state = gaussian(part_keys[0], (PARTICLES, HEIGHT, COLS * CH), 1.0, 6.0, ((0, 4), (1, 4)))
    prev_pred = gaussian(part_keys[1], (PARTICLES, HEIGHT, COLS * CH), 1.0, 6.0, ((0, 4), (1, 4)))
    ancestors = draw_ancestors(jax.random.fold_in(jax.random.fold_in(key_of[11], part), 71), part)
    timestep = jax.random.randint(part_keys[3], (1,), 50, 950).astype(jnp.int32)
    w_in = gaussian(key_of[4], (2 * CH, D), (2 * CH) ** -0.5, 0.5)
    w_time = gaussian(key_of[5], (D, D), D ** -0.5, 0.375)
    w_qkv = gaussian(key_of[6], (BLOCKS, D, 3 * D), D ** -0.5, 0.375)
    w_attn_out = gaussian(key_of[7], (BLOCKS, D, D), D ** -0.5, 0.375)
    w_up = gaussian(key_of[8], (BLOCKS, D, FF), D ** -0.5, 0.375)
    w_down = gaussian(key_of[9], (BLOCKS, FF, D), FF ** -0.5, 0.1875)
    w_out = gaussian(key_of[10], (D, CH), D ** -0.5, 0.375)
    return {"state": state, "prev_pred": prev_pred, "ancestors": ancestors, "timestep": timestep, "w_in": w_in, "w_time": w_time, "w_qkv": w_qkv, "w_attn_out": w_attn_out, "w_up": w_up, "w_down": w_down, "w_out": w_out}


def rms_round(values_in):
    widened = values_in.astype(jnp.float32)
    scaled = widened * lax.rsqrt(lax.optimization_barrier(jnp.mean(widened * widened, axis=-1, keepdims=True)) + 1e-06)
    return scaled.astype(jnp.bfloat16)

def unit_rows(values_in):
    return values_in * lax.rsqrt(lax.optimization_barrier(jnp.mean(values_in * values_in, axis=-1, keepdims=True)) + 1e-06)

def rotate(values_in, span_len):
    half_size = values_in.shape[-1] // 2
    places = jnp.arange(span_len, dtype=jnp.float32)
    rates = jnp.exp(-math.log(10000.0) * jnp.arange(half_size, dtype=jnp.float32) / half_size)
    angles = places[:, None] * rates[None, :]
    cos_part = jnp.cos(angles)[:, None, None, :]
    sin_part = jnp.sin(angles)[:, None, None, :]
    leading = values_in[..., :half_size]
    trailing = values_in[..., half_size:]
    return jnp.concatenate([leading * cos_part - trailing * sin_part, leading * sin_part + trailing * cos_part], axis=-1)

def attend(normed, weight_qkv, weight_out):
    batch_size, span_len, side_len, model_width = normed.shape
    head_size = model_width // HEADS
    joined = jnp.dot(normed, weight_qkv, preferred_element_type=jnp.float32)
    queries = unit_rows(joined[..., :model_width]).reshape(batch_size, span_len, side_len, HEADS, head_size)
    key_rows = unit_rows(joined[..., model_width:2 * model_width]).reshape(batch_size, span_len, side_len, HEADS, head_size)
    values = joined[..., 2 * model_width:].astype(jnp.bfloat16).reshape(batch_size, span_len, side_len, HEADS, head_size)
    queries = rotate(queries, span_len).astype(jnp.bfloat16)
    key_rows = rotate(key_rows, span_len).astype(jnp.bfloat16)
    scores = jnp.einsum('blmhe,bkmhe->bmhlk', queries.astype(jnp.float32), key_rows.astype(jnp.float32)) / math.sqrt(head_size)
    weights = jnp.exp(scores)
    shares = (weights / lax.optimization_barrier(jnp.sum(weights, axis=-1, keepdims=True))).astype(jnp.bfloat16)
    mixture = jnp.einsum('bmhlk,bkmhe->blmhe', shares.astype(jnp.float32), values.astype(jnp.float32))
    mixture = mixture.astype(jnp.bfloat16).reshape(batch_size, span_len, side_len, model_width)
    return jnp.dot(mixture, weight_out, preferred_element_type=jnp.float32)

def mix_tokens(hidden, weight_qkv, weight_out):
    return (hidden.astype(jnp.float32) + attend(rms_round(hidden), weight_qkv, weight_out)).astype(jnp.bfloat16)

def feed_forward(hidden, weight_up, weight_down):
    lifted = jnp.dot(rms_round(hidden), weight_up, preferred_element_type=jnp.float32)
    gated = jax.nn.gelu(lifted, approximate=True).astype(jnp.bfloat16)
    return (hidden.astype(jnp.float32) + jnp.dot(gated, weight_down, preferred_element_type=jnp.float32)).astype(jnp.bfloat16)

def level(moment):
    cosine = jnp.cos((moment / STEPS + 0.008) / 1.008 * math.pi / 2.0)
    return cosine * cosine

def time_vector(timestep, w_time):
    moment = timestep[0].astype(jnp.float32)
    half_size = w_time.shape[0] // 2
    rates = jnp.exp(-math.log(10000.0) * jnp.arange(half_size, dtype=jnp.float32) / half_size)
    embedded = jnp.concatenate([jnp.sin(moment * rates), jnp.cos(moment * rates)])
    return jnp.dot(embedded, w_time.astype(jnp.float32), precision=lax.Precision.HIGHEST)

def reference(state, prev_pred, ancestors, timestep, w_in, w_time, w_qkv, w_attn_out, w_up, w_down, w_out):
    offset_vec = time_vector(timestep, w_time)
    moment = timestep[0].astype(jnp.float32)
    level_now = level(moment)
    level_next = level(moment - STRIDE)
    chosen_state = jnp.take(state, ancestors, axis=0)
    chosen_prev = jnp.take(prev_pred, ancestors, axis=0)

    def denoise(pieces):
        state_rows, prev_rows = pieces
        height_len = state_rows.shape[0]
        joined = jnp.concatenate([state_rows.reshape(height_len, COLS, CH), prev_rows.reshape(height_len, COLS, CH)], axis=-1)
        hidden = (jnp.dot(joined, w_in, preferred_element_type=jnp.float32) + offset_vec).astype(jnp.bfloat16)
        hidden = hidden[:, :, None, :]
        hidden = mix_tokens(hidden, w_qkv[0], w_attn_out[0])
        hidden = feed_forward(hidden, w_up[0], w_down[0])
        hidden = hidden.reshape(1, height_len, COLS, hidden.shape[-1])
        hidden = mix_tokens(hidden, w_qkv[1], w_attn_out[1])
        hidden = feed_forward(hidden, w_up[1], w_down[1])
        predicted = jnp.dot(rms_round(hidden), w_out, preferred_element_type=jnp.float32).astype(jnp.bfloat16)
        predicted = predicted.reshape(height_len, COLS * CH)
        widened = state_rows.astype(jnp.float32)
        pred_wide = predicted.astype(jnp.float32)
        noise_est = (widened - jnp.sqrt(level_now) * pred_wide) / jnp.sqrt(1.0 - level_now)
        updated = (jnp.sqrt(level_next) * pred_wide + jnp.sqrt(1.0 - level_next) * noise_est).astype(jnp.bfloat16)
        return (updated, predicted)
    new_state, new_pred = lax.map(denoise, (chosen_state, chosen_prev))
    return (new_state, new_pred)
```

```python
import functools
import math

import jax
import jax.numpy as jnp
import numpy as np
from jax import lax
from jax.experimental import pallas as pl
from jax.experimental.pallas import tpu as pltpu
from jax.sharding import PartitionSpec as P

HEADS = 8
STEPS = 1000
STRIDE = 20
LANES = 128
MESH = pl.DeviceIdType.MESH
F32 = jnp.float32
BF16 = jnp.bfloat16


def rms(v):
    return v * lax.rsqrt(jnp.mean(v * v, axis=-1, keepdims=True) + 1e-06)


def mm(a, b):
    return jnp.dot(a, b, preferred_element_type=F32)


def mm_nt(a, b):
    return lax.dot_general(a, b, (((1,), (1,)), ((), ())), preferred_element_type=F32)


def rope_tables(length, head, lanes):
    half = head // 2
    rates = np.exp(-math.log(10000.0) * np.arange(half) / half)
    angles = np.tile(np.arange(length)[:, None] * rates[None, :], (1, lanes // half))
    return np.cos(angles).astype(np.float32), np.sin(angles).astype(np.float32)


def halves_first(d, head):
    half = head // 2
    new = np.arange(d)
    old = (new % (d // 2)) // half * head + new // (d // 2) * half + new % half
    return (np.arange(d)[:, None] == old[None, :]).astype(np.float32)


def rotated(v, cos, sin, scale=1.0):
    a, c = v[:, : v.shape[1] // 2], v[:, v.shape[1] // 2 :]
    inv = lax.rsqrt(jnp.mean(v * v, axis=-1, keepdims=True) + 1e-06) * scale
    return jnp.concatenate([(a * cos - c * sin) * inv, (a * sin + c * cos) * inv], axis=1)


def attention(q, k, v, mask, head):
    n, d = q.shape
    lane = lax.broadcasted_iota(jnp.int32, (1, LANES), 1)
    wide_lane = lax.broadcasted_iota(jnp.int32, (1, d), 1) % (d // 2)
    per = LANES // head
    outs = []
    for part in range(len(v)):
        keys, vals = [], []
        for h in range(per):
            pick = jnp.where(lane // head == h, 1.0, 0.0).astype(BF16)
            pick_key = jnp.where(wide_lane // (head // 2) == part * per + h, 1.0, 0.0).astype(BF16)
            keys.append(k * pick_key)
            vals.append(
                jnp.concatenate([v[part] * pick, jnp.broadcast_to(pick, (n, LANES))], axis=1)
            )
        scores = mm_nt(q, jnp.concatenate(keys, axis=0))
        weights = jnp.exp2(scores.astype(BF16))
        if mask is not None:
            weights = weights * mask
        both = mm(weights, jnp.concatenate(vals, axis=0))
        outs.append(both[:, :LANES] / both[:, LANES:])
    return jnp.concatenate(outs, axis=1).astype(BF16)


def mlp(h, w_up, w_down):
    x = mm(rms(h).astype(BF16), w_up).astype(BF16)
    root = math.sqrt(2.0 / math.pi)
    inner = x * (root + (root * 0.044715) * (x * x))
    gated = x + x * jnp.tanh(inner)
    return (h + 0.5 * mm(gated, w_down)).astype(BF16)


def kernel(
    cfg,
    anc_hbm, time_hbm, state_hbm, prev_hbm, tab_hbm, perm_hbm, w_in_hbm, w_time_hbm,
    w_qkv_hbm, w_attn_hbm, w_up_hbm, w_down_hbm, w_out_hbm,
    state_out, pred_out,
    anc_ref, time_ref, state_ref, prev_ref, tab_ref, perm_ref, w_in_ref, w_time_ref, w_out_ref,
    w_qkv, w_attn, w_up, w_down,
    xs, xp, h1, hcol, q2, k2, v2, ptok, flats, sel, fin, spair, ssel, sfin,
    in_sem, w_sem, own_sem, sa_send, sa_recv, sb_send, sb_recv, h_send, h_recv, p_send, p_recv,
):
    ndom, nrow, rows, cols, ch, d, head, height, wide, flat, pair = cfg
    dom, row = lax.axis_index("dom"), lax.axis_index("row")
    mine = cols // nrow
    group = LANES // math.gcd(ch, LANES)
    glanes = group * ch
    held = mine // pair
    halves = held // wide
    scale = math.log2(math.e) / math.sqrt(head)
    teams = ndom // pair
    team, seat = lax.div(dom, pair), lax.rem(dom, pair)

    def fetch(i, src, dst):
        copy = pltpu.make_async_copy(src, dst, in_sem.at[i])
        copy.start()
        return copy

    got_state = [fetch(0, state_hbm, state_ref), fetch(1, prev_hbm, prev_ref)]
    got_time = [
        fetch(2, time_hbm, time_ref), fetch(3, tab_hbm, tab_ref), fetch(4, w_time_hbm, w_time_ref),
        fetch(5, w_in_hbm, w_in_ref), fetch(8, perm_hbm, perm_ref),
    ]

    loads = []
    pairs = ((w_qkv_hbm, w_qkv), (w_attn_hbm, w_attn), (w_up_hbm, w_up), (w_down_hbm, w_down))
    for b in range(2):
        for i, (src, dst) in enumerate(pairs):
            copy = pltpu.make_async_copy(src.at[b], dst.at[b], w_sem.at[b, i])
            copy.start()
            loads.append(copy)

    barrier = pltpu.get_barrier_semaphore()

    def greet(i, carry):
        pl.semaphore_signal(
            barrier,
            inc=1,
            device_id={"dom": lax.rem(dom + lax.div(i, nrow), ndom), "row": lax.rem(row + lax.rem(i, nrow), nrow)},
            device_id_type=MESH,
        )
        return carry

    lax.fori_loop(1, ndom * nrow, greet, 0, unroll=ndom * nrow <= 16)
    got_late = [fetch(6, anc_hbm, anc_ref), fetch(7, w_out_hbm, w_out_ref)]
    for copy in got_state:
        copy.wait()
    own = pltpu.make_async_copy(state_ref.at[0], spair.at[seat], own_sem)
    own.start()

    lane = lax.broadcasted_iota(jnp.int32, (rows, LANES), 1)

    def split(c, carry):
        base = pl.multiple_of(c * glanes, LANES)
        for ref, out in ((state_ref, xs), (prev_ref, xp)):
            tiles = [
                ref[0, :, pl.ds(pl.multiple_of(base + j * LANES, LANES), LANES)].astype(F32)
                for j in range(glanes // LANES)
            ]
            for t in range(group):
                j, off = divmod(t * ch, LANES)
                v = pltpu.roll(tiles[j], LANES - off, 1) if off else tiles[j]
                if off + ch > LANES:
                    v = jnp.where(lane < LANES - off, v, pltpu.roll(tiles[j + 1], LANES - off, 1))
                out[pl.ds(c * group + t, rows, stride=cols), :] = v
        return carry

    lax.fori_loop(0, cols // group, split, 0)

    for copy in got_time:
        copy.wait()
    moment = time_ref[0].astype(F32)
    half = d // 2
    times = jnp.broadcast_to(moment, (1, LANES))
    now, nxt = level(times), level(times - STRIDE)
    c1, c2 = jnp.sqrt(now), jnp.sqrt(nxt)
    c3 = jnp.sqrt(1.0 - nxt) / jnp.sqrt(1.0 - now)
    angles = tab_ref[2 * cols + 16 * height :, :] * moment
    emb = jnp.concatenate([jnp.sin(angles), jnp.cos(angles)], axis=1)
    temb = jnp.dot(
        emb, w_time_ref[...].astype(F32),
        precision=lax.Precision.HIGHEST, preferred_element_type=F32,
    )[0:1]
    w_in = w_in_ref[...].astype(F32)
    gap = jnp.zeros((LANES - ch, d), F32)
    w_in = jnp.concatenate([w_in[:ch], gap, w_in[ch:], gap], axis=0).astype(BF16)

    for copy in loads[:4]:
        copy.wait()

    def halve(b):
        for i in range(2):
            at = slice(i * d, (i + 1) * d)
            w_qkv[b, :, at] = mm(w_qkv[b, :, at], perm_ref[...]).astype(BF16)

    halve(0)
    cos_r, sin_r = tab_ref[0:cols], tab_ref[cols : 2 * cols]
    step_rows = 2 if rows % 2 == 0 else 1
    n0 = step_rows * cols

    others = [(e, k) for e in range(pair) for k in range(nrow) if (e, k) != (0, 0)]

    def h_copy(i, e, k):
        peer, place = lax.rem(row + k, nrow), lax.rem(seat + e, pair)
        span = pl.ds(i * step_rows, step_rows)
        return pltpu.make_async_remote_copy(
            src_ref=h1.at[peer, place, span],
            dst_ref=hcol.at[seat, row, span],
            send_sem=h_send.at[i, e, k],
            recv_sem=h_recv.at[i, e, k],
            device_id={"dom": team * pair + place, "row": peer},
            device_id_type=MESH,
        )

    def state_pair(e):
        return pltpu.make_async_remote_copy(
            src_ref=state_ref.at[0],
            dst_ref=spair.at[seat],
            send_sem=sa_send.at[e],
            recv_sem=sa_recv.at[e],
            device_id={"dom": team * pair + lax.rem(seat + e, pair)},
            device_id_type=MESH,
        )

    def state_team(e):
        there = lax.rem(team + e, teams)
        return pltpu.make_async_remote_copy(
            src_ref=ssel.at[there],
            dst_ref=sfin.at[team],
            send_sem=sb_send.at[e],
            recv_sem=sb_recv.at[e],
            device_id={"dom": there * pair + seat},
            device_id_type=MESH,
        )

    def pick(there):
        return jnp.clip(anc_ref[there] - team * pair, 0, pair - 1)

    def first(i):
        sl = pl.ds(i * n0, n0)
        x = jnp.concatenate([xs[sl, :].astype(BF16), xp[sl, :].astype(BF16)], axis=1)
        h = mm(x, w_in) + temb
        h = h.astype(BF16).astype(F32)
        qkv = mm(rms(h).astype(BF16), w_qkv[0])
        cos = jnp.concatenate([cos_r] * step_rows, axis=0)
        sin = jnp.concatenate([sin_r] * step_rows, axis=0)
        q = rotated(qkv[:, :d], cos, sin, scale).astype(BF16)
        k = rotated(qkv[:, d : 2 * d], cos, sin).astype(BF16)
        v = qkv[:, 2 * d :].astype(BF16)
        v = [v[:, p * LANES : (p + 1) * LANES] for p in range(d // LANES)]
        mixed = []
        for r in range(step_rows):
            a, b = r * cols, (r + 1) * cols
            mixed.append(
                attention(q[a:b], k[a:b], [x[a:b] for x in v], None, head)
            )
        o = jnp.concatenate(mixed, axis=0)
        h = (h + mm(o, w_attn[0])).astype(BF16).astype(F32)
        h = mlp(h, w_up[0], w_down[0])
        h = h.reshape(step_rows, cols, d)
        span = slice(i * step_rows, (i + 1) * step_rows)
        for g in range(nrow * pair):
            h1[g // pair, g % pair, span] = h[:, g * held : (g + 1) * held, :]

    pl.semaphore_wait(barrier, ndom * nrow - 1)
    for e in range(1, pair):
        state_pair(e).start()
    for i in range(rows // step_rows):
        first(i)
        for e, k in others:
            h_copy(i, e, k).start()

    for copy in loads[4:] + got_late:
        copy.wait()
    own.wait()
    for e in range(1, pair):
        state_pair(e).wait_recv()
    for e in range(1, teams):
        there = lax.rem(team + e, teams)
        ssel[there] = spair[pick(there * pair + seat)]
        state_team(e).start()
    sfin[team] = spair[pick(dom)]

    hcol[seat, row] = h1[row, seat]
    halve(1)

    cos_c = tab_ref[2 * cols : 2 * cols + 8 * height].reshape(height, 8, LANES)
    sin_c = tab_ref[2 * cols + 8 * height : 2 * cols + 16 * height].reshape(height, 8, LANES)
    cos_c = jnp.concatenate([cos_c] * (held // 8), axis=1).reshape(nrow, rows, held, LANES)
    sin_c = jnp.concatenate([sin_c] * (held // 8), axis=1).reshape(nrow, rows, held, LANES)
    sub = height * wide
    n1 = pair * sub
    n2 = pair * nrow * step_rows * held
    per = LANES // head
    qi = lax.broadcasted_iota(jnp.int32, (sub, per * sub), 0)
    ki = lax.broadcasted_iota(jnp.int32, (sub, per * sub), 1)
    mask = jnp.where(qi % wide == ki % wide, 1.0, 0.0).astype(BF16)
    hlane = lax.broadcasted_iota(jnp.int32, (height, LANES), 1)

    def project(i):
        span = slice(i * step_rows, (i + 1) * step_rows)
        h = hcol[:, :, span].reshape(n2, d).astype(F32)
        qkv = mm(rms(h).astype(BF16), w_qkv[1])
        cos = jnp.concatenate([cos_c[:, span].reshape(n2 // pair, LANES)] * pair, axis=0)
        sin = jnp.concatenate([sin_c[:, span].reshape(n2 // pair, LANES)] * pair, axis=0)
        shape = (pair, nrow, step_rows, held, d)
        q2[:, :, span] = rotated(qkv[:, :d], cos, sin, scale).reshape(shape)
        k2[:, :, span] = rotated(qkv[:, d : 2 * d], cos, sin).reshape(shape)
        v2[:, :, span] = qkv[:, 2 * d :].reshape(shape)

    for i in range(rows // step_rows):
        for e, k in others:
            h_copy(i, e, k).wait_recv()
        project(i)

    def second(s):
        span = slice(s * wide, (s + 1) * wide)
        mixed = []
        for p in range(pair):
            q, k, v = (x[p, :, :, span, :].reshape(sub, d).astype(BF16) for x in (q2, k2, v2))
            v = [v[:, t * LANES : (t + 1) * LANES] for t in range(d // LANES)]
            mixed.append(attention(q, k, v, mask, head))
        o = jnp.concatenate(mixed, axis=0)
        h = hcol[...].astype(F32)[:, :, :, span, :].reshape(n1, d)
        h = (h + mm(o, w_attn[1])).astype(BF16).astype(F32)
        h = mlp(h, w_up[1], w_down[1]).astype(F32)
        ptok[:, 0:ch] = mm_nt(rms(h).astype(BF16), w_out_ref[...])
        for p in range(pair):
            toks = [ptok[pl.ds(p * sub + t, height, stride=wide), :] for t in range(wide)]
            for j in range(flat // LANES):
                first_t = (j * LANES) // ch
                last_t = min((j * LANES + LANES - 1) // ch, wide - 1)
                acc = None
                for t in range(first_t, last_t + 1):
                    at = t * ch - j * LANES
                    x = pltpu.roll(toks[t], at % LANES, 1) if at % LANES else toks[t]
                    acc = x if acc is None else jnp.where(hlane >= at, x, acc)
                flats[p, :, j * LANES : (j + 1) * LANES] = acc
        for there in range(ndom):
            want = pick(there)
            for r in range(nrow):
                sel[s, there, r] = flats[want, r * rows : (r + 1) * rows, :].astype(BF16)

    def p_copy(s, e, k):
        there, peer = lax.rem(dom + e, ndom), lax.rem(row + k, nrow)
        return pltpu.make_async_remote_copy(
            src_ref=sel.at[s, there, peer],
            dst_ref=fin.at[s, team, row, seat],
            send_sem=p_send.at[s, e, k],
            recv_sem=p_recv.at[s, e, k],
            device_id={"dom": there, "row": peer},
            device_id_type=MESH,
        )

    targets = [(e, k) for e in range(ndom) for k in range(nrow) if (e, k) != (0, 0)]
    for s in range(halves):
        second(s)
        for e, k in targets:
            p_copy(s, e, k).start()
        fin[s, team, row, seat] = sel[s, dom, row]

    for e in range(1, teams):
        state_team(e).wait_recv()
    home = lax.div(anc_ref[dom], pair)

    for s in range(halves):
        for e, k in targets:
            p_copy(s, e, k).wait_recv()

    size = wide * ch
    count = flat // LANES

    def piece(q, offset):
        g, s = divmod(q, halves)
        tile, rem = divmod(offset, LANES)

        def load(j):
            x = fin[s, home, g // pair, g % pair, :, j * LANES : (j + 1) * LANES].astype(F32)
            return pltpu.roll(x, LANES - rem, 1) if rem else x

        low = load(tile) if tile >= 0 else None
        if not rem or tile + 1 >= count:
            return low
        high = load(tile + 1)
        return high if low is None else jnp.where(lane < LANES - rem, low, high)

    for j in range(cols * ch // LANES):
        start = j * LANES
        acc = None
        for q in range(start // size, (start + LANES - 1) // size + 1):
            x = piece(q, start - q * size)
            acc = x if acc is None else jnp.where(lane >= q * size - start, x, acc)
        acc = acc.astype(BF16)
        pred_out[0, :, start : start + LANES] = acc
        pred = acc.astype(F32)
        old = sfin[home, :, start : start + LANES].astype(F32)
        state_out[0, :, start : start + LANES] = (c2 * pred + c3 * (old - c1 * pred)).astype(BF16)

    for e in range(1, pair):
        state_pair(e).wait_send()
    for e in range(1, teams):
        state_team(e).wait_send()
    for i in range(rows // step_rows):
        for e, k in others:
            h_copy(i, e, k).wait_send()
    for s in range(halves):
        for e, k in targets:
            p_copy(s, e, k).wait_send()


def level(moment):
    cosine = jnp.cos((moment / STEPS + 0.008) / 1.008 * math.pi / 2.0)
    return cosine * cosine


def hand_out(state_ref, pred_ref, new_state_ref, new_pred_ref, sems):
    first = pltpu.make_async_copy(state_ref, new_state_ref, sems.at[0])
    second = pltpu.make_async_copy(pred_ref, new_pred_ref, sems.at[1])
    first.start()
    second.start()
    first.wait()
    second.wait()


def per_device(
    sizes, state, prev_pred, ancestors, timestep, w_in, w_time, w_qkv, w_attn_out, w_up, w_down, w_out
):
    ndom, nrow = sizes
    _, rows, width = state.shape
    d, ch = w_out.shape
    cols, height, head = width // ch, rows * nrow, d // HEADS
    ff = w_up.shape[2]
    half = d // 2
    rates = np.exp(-math.log(10000.0) * np.arange(half) / half).astype(np.float32)
    cos_r, sin_r = rope_tables(cols, head, LANES)
    cos_c, sin_c = rope_tables(height, head, LANES)
    tables = jnp.asarray(
        np.concatenate(
            [
                cos_r, sin_r, np.repeat(cos_c, 8, axis=0), np.repeat(sin_c, 8, axis=0),
                np.tile(rates[None], (8, 1)),
            ]
        )
    )
    perm = jnp.asarray(halves_first(d, head).astype(jnp.bfloat16))
    mine = cols // nrow
    wide = min(8, mine)
    pair = max(p for p in range(1, ndom + 1) if ndom % p == 0 and p * p <= ndom and mine % (p * wide) == 0)
    teams, held = ndom // pair, mine // pair
    flat = -(-wide * ch // LANES) * LANES
    halves, steps = held // wide, max(rows // 2, 1)
    cfg = (ndom, nrow, rows, cols, ch, d, head, height, wide, flat, pair)
    vmem = pl.BlockSpec(memory_space=pltpu.VMEM)
    hbm = pl.BlockSpec(memory_space=pl.ANY)
    whole = jax.ShapeDtypeStruct((1, rows, width), BF16)
    dma = pltpu.SemaphoreType.DMA
    stepped, predicted = pl.pallas_call(
        functools.partial(kernel, cfg),
        out_shape=(pltpu.VMEM((1, rows, width), BF16),) * 2,
        in_specs=[hbm] * 13,
        out_specs=(vmem, vmem),
        scratch_shapes=[
            pltpu.SMEM(ancestors.shape, jnp.int32),
            pltpu.SMEM(timestep.shape, jnp.int32),
            pltpu.VMEM(state.shape, BF16),
            pltpu.VMEM(state.shape, BF16),
            pltpu.VMEM(tables.shape, F32),
            pltpu.VMEM(perm.shape, BF16),
            pltpu.VMEM(w_in.shape, BF16),
            pltpu.VMEM(w_time.shape, BF16),
            pltpu.VMEM((ch, d), BF16),
            pltpu.VMEM((2, d, 3 * d), BF16),
            pltpu.VMEM((2, d, d), BF16),
            pltpu.VMEM((2, d, ff), BF16),
            pltpu.VMEM((2, ff, d), BF16),
            pltpu.VMEM((rows * cols, LANES), F32),
            pltpu.VMEM((rows * cols, LANES), F32),
            pltpu.VMEM((nrow, pair, rows, held, d), BF16),
            pltpu.VMEM((pair, nrow, rows, held, d), BF16),
            *[pltpu.VMEM((pair, nrow, rows, held, d), F32)] * 3,
            pltpu.VMEM((pair * height * wide, LANES), F32),
            pltpu.VMEM((pair, height, flat), F32),
            pltpu.VMEM((halves, ndom, nrow, rows, flat), BF16),
            pltpu.VMEM((halves, teams, nrow, pair, rows, flat), BF16),
            pltpu.VMEM((pair, rows, width), BF16),
            pltpu.VMEM((teams, rows, width), BF16),
            pltpu.VMEM((teams, rows, width), BF16),
            dma((9,)),
            dma((2, 4)),
            dma,
            dma((pair,)),
            dma((pair,)),
            dma((teams,)),
            dma((teams,)),
            dma((steps, pair, nrow)),
            dma((steps, pair, nrow)),
            dma((halves, ndom, nrow)),
            dma((halves, ndom, nrow)),
        ],
        compiler_params=pltpu.CompilerParams(
            collective_id=0, has_side_effects=True, vmem_limit_bytes=56 * 1024 * 1024,
        ),
    )(
        ancestors, timestep, state, prev_pred, tables, perm, w_in, w_time,
        w_qkv, w_attn_out, w_up, w_down, w_out.T,
    )
    return pl.pallas_call(
        hand_out,
        out_shape=(whole, whole),
        in_specs=[vmem, vmem],
        out_specs=(hbm, hbm),
        scratch_shapes=[dma((2,))],
        compiler_params=pltpu.CompilerParams(vmem_limit_bytes=4 * 1024 * 1024),
    )(stepped, predicted)


def solution(mesh):
    part = P(("group", "dom"), "row", None)
    in_specs = (part, part, P("group"), P("group")) + (P(),) * 7
    return jax.shard_map(
        functools.partial(per_device, (mesh.shape["dom"], mesh.shape["row"])),
        mesh=mesh, in_specs=in_specs, out_specs=(part, part), check_vma=False,
    )
```

```python
import functools
import math

import jax
import jax.numpy as jnp
import numpy as np
from jax import lax
from jax.experimental import pallas as pl
from jax.experimental.pallas import tpu as pltpu
from jax.sharding import PartitionSpec as P

HEADS = 8
STEPS = 1000
STRIDE = 20
LANES = 128
MESH = pl.DeviceIdType.MESH
F32 = jnp.float32
BF16 = jnp.bfloat16


def rms(v):
    return v * lax.rsqrt(jnp.mean(v * v, axis=-1, keepdims=True) + 1e-06)


def mm(a, b):
    return jnp.dot(a, b, preferred_element_type=F32)


def mm_nt(a, b):
    return lax.dot_general(a, b, (((1,), (1,)), ((), ())), preferred_element_type=F32)


def rope_tables(length, head, lanes):
    half = head // 2
    rates = np.exp(-math.log(10000.0) * np.arange(half) / half)
    angles = np.tile(np.arange(length)[:, None] * rates[None, :], (1, lanes // half))
    return np.cos(angles).astype(np.float32), np.sin(angles).astype(np.float32)


def halves_first(d, head):
    half = head // 2
    new = np.arange(d)
    old = (new % (d // 2)) // half * head + new // (d // 2) * half + new % half
    return (np.arange(d)[:, None] == old[None, :]).astype(np.float32)


def rotated(v, cos, sin, scale=1.0):
    a, c = v[:, : v.shape[1] // 2], v[:, v.shape[1] // 2 :]
    inv = lax.rsqrt(jnp.mean(v * v, axis=-1, keepdims=True) + 1e-06) * scale
    return jnp.concatenate([(a * cos - c * sin) * inv, (a * sin + c * cos) * inv], axis=1)


def attention(q, k, v, mask, head):
    n, d = q.shape
    lane = lax.broadcasted_iota(jnp.int32, (1, LANES), 1)
    wide_lane = lax.broadcasted_iota(jnp.int32, (1, d), 1) % (d // 2)
    per = LANES // head
    outs = []
    for part in range(len(v)):
        keys, vals = [], []
        for h in range(per):
            pick = jnp.where(lane // head == h, 1.0, 0.0).astype(BF16)
            pick_key = jnp.where(wide_lane // (head // 2) == part * per + h, 1.0, 0.0).astype(BF16)
            keys.append(k * pick_key)
            vals.append(
                jnp.concatenate([v[part] * pick, jnp.broadcast_to(pick, (n, LANES))], axis=1)
            )
        scores = mm_nt(q, jnp.concatenate(keys, axis=0))
        weights = jnp.exp2(scores.astype(BF16))
        if mask is not None:
            weights = weights * mask
        both = mm(weights, jnp.concatenate(vals, axis=0))
        outs.append(both[:, :LANES] / both[:, LANES:])
    return jnp.concatenate(outs, axis=1).astype(BF16)


def mlp(h, w_up, w_down):
    x = mm(rms(h).astype(BF16), w_up).astype(BF16)
    root = math.sqrt(2.0 / math.pi)
    inner = x * (root + (root * 0.044715) * (x * x))
    gated = x + x * jnp.tanh(inner)
    return (h + 0.5 * mm(gated, w_down)).astype(BF16)


def kernel(
    cfg,
    anc_hbm, time_hbm, state_hbm, prev_hbm, tab_hbm, perm_hbm, w_in_hbm, w_time_hbm,
    w_qkv_hbm, w_attn_hbm, w_up_hbm, w_down_hbm, w_out_hbm,
    state_out, pred_out,
    anc_ref, time_ref, state_ref, prev_ref, tab_ref, perm_ref, w_in_ref, w_time_ref, w_out_ref,
    w_qkv, w_attn, w_up, w_down,
    xs, xp, h1, hcol, q2, k2, v2, ptok, flats, sel, fin, spair, ssel, sfin,
    in_sem, w_sem, own_sem, sa_send, sa_recv, sb_send, sb_recv, h_send, h_recv, p_send, p_recv,
):
    ndom, nrow, rows, cols, ch, d, head, height, wide, flat, pair = cfg
    dom, row = lax.axis_index("dom"), lax.axis_index("row")
    mine = cols // nrow
    group = LANES // math.gcd(ch, LANES)
    glanes = group * ch
    held = mine // pair
    halves = held // wide
    scale = math.log2(math.e) / math.sqrt(head)
    teams = ndom // pair
    team, seat = lax.div(dom, pair), lax.rem(dom, pair)

    def fetch(i, src, dst):
        copy = pltpu.make_async_copy(src, dst, in_sem.at[i])
        copy.start()
        return copy

    got_state = [fetch(0, state_hbm, state_ref), fetch(1, prev_hbm, prev_ref)]
    got_time = [
        fetch(2, time_hbm, time_ref), fetch(3, tab_hbm, tab_ref), fetch(4, w_time_hbm, w_time_ref),
        fetch(5, w_in_hbm, w_in_ref), fetch(8, perm_hbm, perm_ref),
    ]

    pairs = ((w_qkv_hbm, w_qkv), (w_attn_hbm, w_attn), (w_up_hbm, w_up), (w_down_hbm, w_down))

    def load(b, i):
        src, dst = pairs[i]
        copy = pltpu.make_async_copy(src.at[b], dst.at[b], w_sem.at[b, i])
        copy.start()
        return copy

    got_time.append(load(0, 0))
    barrier = pltpu.get_barrier_semaphore()

    def greet(i, carry):
        pl.semaphore_signal(
            barrier,
            inc=1,
            device_id={"dom": lax.rem(dom + lax.div(i, nrow), ndom), "row": lax.rem(row + lax.rem(i, nrow), nrow)},
            device_id_type=MESH,
        )
        return carry

    lax.fori_loop(1, ndom * nrow, greet, 0, unroll=ndom * nrow <= 16)
    loads = [load(0, i) for i in range(1, 4)]
    got_late = [load(1, i) for i in range(4)]
    got_late += [fetch(6, anc_hbm, anc_ref), fetch(7, w_out_hbm, w_out_ref)]
    for copy in got_state + got_time:
        copy.wait()
    own = pltpu.make_async_copy(state_ref.at[0], spair.at[seat], own_sem)
    own.start()

    pitch = xs.shape[0] // rows
    lane = lax.broadcasted_iota(jnp.int32, (rows, LANES), 1)

    def split(c, carry):
        base = pl.multiple_of(c * glanes, LANES)
        for ref, out in ((state_ref, xs), (prev_ref, xp)):
            tiles = [
                ref[0, :, pl.ds(pl.multiple_of(base + j * LANES, LANES), LANES)].astype(F32)
                for j in range(glanes // LANES)
            ]
            for t in range(group):
                j, off = divmod(t * ch, LANES)
                v = pltpu.roll(tiles[j], LANES - off, 1) if off else tiles[j]
                if off + ch > LANES:
                    v = jnp.where(lane < LANES - off, v, pltpu.roll(tiles[j + 1], LANES - off, 1))
                out[pl.ds(c * group + t, rows, stride=pitch), :] = v
        return carry

    lax.fori_loop(0, cols // group, split, 0, unroll=True)

    moment = time_ref[0].astype(F32)
    half = d // 2
    times = jnp.broadcast_to(moment, (1, LANES))
    now, nxt = level(times), level(times - STRIDE)
    c1, c2 = jnp.sqrt(now), jnp.sqrt(nxt)
    c3 = jnp.sqrt(1.0 - nxt) / jnp.sqrt(1.0 - now)
    angles = tab_ref[2 * cols + 16 * height :, :] * moment
    emb = jnp.concatenate([jnp.sin(angles), jnp.cos(angles)], axis=1)
    temb = jnp.dot(
        emb, w_time_ref[...].astype(F32),
        precision=lax.Precision.HIGHEST, preferred_element_type=F32,
    )[0:1]
    w_in = w_in_ref[...].astype(F32)
    gap = jnp.zeros((LANES - ch, d), F32)
    w_in = jnp.concatenate([w_in[:ch], gap, w_in[ch:], gap], axis=0).astype(BF16)

    def halve(b):
        for i in range(2):
            at = slice(i * d, (i + 1) * d)
            w_qkv[b, :, at] = mm(w_qkv[b, :, at], perm_ref[...]).astype(BF16)

    halve(0)
    for copy in loads:
        copy.wait()
    cos_r, sin_r = tab_ref[0:cols], tab_ref[cols : 2 * cols]
    step_rows = 2 if rows % 2 == 0 else 1

    others = [(e, k) for e in range(pair - 1, -1, -1) for k in range(nrow - 1, -1, -1) if (e, k) != (0, 0)]

    def h_copy(i, e, k):
        peer, place = lax.rem(row + k, nrow), lax.rem(seat + e, pair)
        span = pl.ds(i * step_rows, step_rows)
        return pltpu.make_async_remote_copy(
            src_ref=h1.at[peer, place, span],
            dst_ref=hcol.at[seat, row, span],
            send_sem=h_send.at[i, e, k],
            recv_sem=h_recv.at[i, e, k],
            device_id={"dom": team * pair + place, "row": peer},
            device_id_type=MESH,
        )

    def state_pair(e):
        return pltpu.make_async_remote_copy(
            src_ref=state_ref.at[0],
            dst_ref=spair.at[seat],
            send_sem=sa_send.at[e],
            recv_sem=sa_recv.at[e],
            device_id={"dom": team * pair + lax.rem(seat + e, pair)},
            device_id_type=MESH,
        )

    def state_team(e):
        there = lax.rem(team + e, teams)
        return pltpu.make_async_remote_copy(
            src_ref=ssel.at[there],
            dst_ref=sfin.at[team],
            send_sem=sb_send.at[e],
            recv_sem=sb_recv.at[e],
            device_id={"dom": there * pair + seat},
            device_id_type=MESH,
        )

    def pick(there):
        return jnp.clip(anc_ref[there] - team * pair, 0, pair - 1)

    def front(i):
        x = jnp.concatenate(
            [
                jnp.concatenate([v[r * pitch : r * pitch + cols, :].astype(BF16) for v in (xs, xp)], axis=1)
                for r in range(i * step_rows, (i + 1) * step_rows)
            ],
            axis=0,
        )
        h = mm(x, w_in) + temb
        h = h.astype(BF16).astype(F32)
        qkv = mm(rms(h).astype(BF16), w_qkv[0])
        cos = jnp.concatenate([cos_r] * step_rows, axis=0)
        sin = jnp.concatenate([sin_r] * step_rows, axis=0)
        q = rotated(qkv[:, :d], cos, sin, scale).astype(BF16)
        k = rotated(qkv[:, d : 2 * d], cos, sin).astype(BF16)
        v = qkv[:, 2 * d :].astype(BF16)
        v = [v[:, p * LANES : (p + 1) * LANES] for p in range(d // LANES)]
        return h, q, k, v

    def middle(h, q, k, v):
        mixed = []
        for r in range(step_rows):
            a, b = r * cols, (r + 1) * cols
            mixed.append(attention(q[a:b], k[a:b], [x[a:b] for x in v], None, head))
        o = jnp.concatenate(mixed, axis=0)
        return (h + mm(o, w_attn[0])).astype(BF16).astype(F32)

    def back(i, h):
        h = mlp(h, w_up[0], w_down[0]).reshape(step_rows, cols, d)
        span = slice(i * step_rows, (i + 1) * step_rows)
        for g in range(nrow * pair):
            h1[g // pair, g % pair, span] = h[:, g * held : (g + 1) * held, :]

    def send(i):
        for e, k in others:
            h_copy(i, e, k).start()

    def enter():
        pl.semaphore_wait(barrier, ndom * nrow - 1)
        for e in range(1, pair):
            state_pair(e).start()

    made = front(0)
    enter()
    for i in range(rows // step_rows):
        h = middle(*made)
        if i + 1 < rows // step_rows:
            made = front(i + 1)
        back(i, h)
        send(i)

    for copy in got_late:
        copy.wait()

    hcol[seat, row] = h1[row, seat]
    halve(1)

    cos_c = tab_ref[2 * cols : 2 * cols + 8 * height].reshape(height, 8, LANES)
    sin_c = tab_ref[2 * cols + 8 * height : 2 * cols + 16 * height].reshape(height, 8, LANES)
    cos_c = jnp.concatenate([cos_c] * (held // 8), axis=1).reshape(nrow, rows, held, LANES)
    sin_c = jnp.concatenate([sin_c] * (held // 8), axis=1).reshape(nrow, rows, held, LANES)
    sub = height * wide
    n1 = pair * sub
    n2 = pair * nrow * step_rows * held
    per = LANES // head
    qi = lax.broadcasted_iota(jnp.int32, (sub, per * sub), 0)
    ki = lax.broadcasted_iota(jnp.int32, (sub, per * sub), 1)
    mask = jnp.where(qi % wide == ki % wide, 1.0, 0.0).astype(BF16)
    hlane = lax.broadcasted_iota(jnp.int32, (height, LANES), 1)

    def project(i):
        span = slice(i * step_rows, (i + 1) * step_rows)
        h = hcol[:, :, span].reshape(n2, d).astype(F32)
        qkv = mm(rms(h).astype(BF16), w_qkv[1])
        cos = jnp.concatenate([cos_c[:, span].reshape(n2 // pair, LANES)] * pair, axis=0)
        sin = jnp.concatenate([sin_c[:, span].reshape(n2 // pair, LANES)] * pair, axis=0)
        shape = (pair, nrow, step_rows, held, d)
        q2[:, :, span] = rotated(qkv[:, :d], cos, sin, scale).reshape(shape)
        k2[:, :, span] = rotated(qkv[:, d : 2 * d], cos, sin).reshape(shape)
        v2[:, :, span] = qkv[:, 2 * d :].reshape(shape)

    for i in range(rows // step_rows):
        for e, k in others:
            h_copy(i, e, k).wait_recv()
        project(i)
        if i == 0:
            own.wait()
            for e in range(1, pair):
                state_pair(e).wait_recv()
            for e in range(1, teams):
                there = lax.rem(team + e, teams)
                ssel[there] = spair[pick(there * pair + seat)]
                state_team(e).start()
            sfin[team] = spair[pick(dom)]

    def second(s):
        span = slice(s * wide, (s + 1) * wide)
        mixed = []
        for p in range(pair):
            q, k, v = (x[p, :, :, span, :].reshape(sub, d).astype(BF16) for x in (q2, k2, v2))
            v = [v[:, t * LANES : (t + 1) * LANES] for t in range(d // LANES)]
            mixed.append(attention(q, k, v, mask, head))
        o = jnp.concatenate(mixed, axis=0)
        h = hcol[...].astype(F32)[:, :, :, span, :].reshape(n1, d)
        h = (h + mm(o, w_attn[1])).astype(BF16).astype(F32)
        h = mlp(h, w_up[1], w_down[1]).astype(F32)
        ptok[:, 0:ch] = mm_nt(rms(h).astype(BF16), w_out_ref[...])
        for p in range(pair):
            toks = [ptok[pl.ds(p * sub + t, height, stride=wide), :] for t in range(wide)]
            for j in range(flat // LANES):
                first_t = (j * LANES) // ch
                last_t = min((j * LANES + LANES - 1) // ch, wide - 1)
                acc = None
                for t in range(first_t, last_t + 1):
                    at = t * ch - j * LANES
                    x = pltpu.roll(toks[t], at % LANES, 1) if at % LANES else toks[t]
                    acc = x if acc is None else jnp.where(hlane >= at, x, acc)
                flats[p, :, j * LANES : (j + 1) * LANES] = acc
        for there in range(ndom):
            want = pick(there)
            for r in range(nrow):
                sel[s, there, r] = flats[want, r * rows : (r + 1) * rows, :].astype(BF16)

    def p_copy(s, e, k):
        there, peer = lax.rem(dom + e, ndom), lax.rem(row + k, nrow)
        return pltpu.make_async_remote_copy(
            src_ref=sel.at[s, there, peer],
            dst_ref=fin.at[s, team, row, seat],
            send_sem=p_send.at[s, e, k],
            recv_sem=p_recv.at[s, e, k],
            device_id={"dom": there, "row": peer},
            device_id_type=MESH,
        )

    targets = [(e, k) for e in range(ndom) for k in range(nrow) if (e, k) != (0, 0)]
    upper = lax.div(dom, max(ndom // 2, 1))
    later = lax.div(upper + 1, 2)

    def far_first(j):
        return later * j + (1 - later) * (ndom - j)

    for s in range(halves):
        second(s)
        for j in range(1, ndom):
            for k in range(nrow):
                p_copy(s, far_first(j), lax.rem(k + 2, nrow)).start()
        for k in range(1, nrow):
            p_copy(s, 0, k).start()
        fin[s, team, row, seat] = sel[s, dom, row]

    for e in range(1, teams):
        state_team(e).wait_recv()
    home = lax.div(anc_ref[dom], pair)

    for s in range(halves):
        for e, k in targets:
            p_copy(s, e, k).wait_recv()

    size = wide * ch
    count = flat // LANES

    def piece(q, offset):
        g, s = divmod(q, halves)
        tile, rem = divmod(offset, LANES)

        def load(j):
            x = fin[s, home, g // pair, g % pair, :, j * LANES : (j + 1) * LANES].astype(F32)
            return pltpu.roll(x, LANES - rem, 1) if rem else x

        low = load(tile) if tile >= 0 else None
        if not rem or tile + 1 >= count:
            return low
        high = load(tile + 1)
        return high if low is None else jnp.where(lane < LANES - rem, low, high)

    for j in range(cols * ch // LANES):
        start = j * LANES
        acc = None
        for q in range(start // size, (start + LANES - 1) // size + 1):
            x = piece(q, start - q * size)
            acc = x if acc is None else jnp.where(lane >= q * size - start, x, acc)
        acc = acc.astype(BF16)
        pred_out[0, :, start : start + LANES] = acc
        pred = acc.astype(F32)
        old = sfin[home, :, start : start + LANES].astype(F32)
        state_out[0, :, start : start + LANES] = (c2 * pred + c3 * (old - c1 * pred)).astype(BF16)

    for e in range(1, pair):
        state_pair(e).wait_send()
    for e in range(1, teams):
        state_team(e).wait_send()
    for i in range(rows // step_rows):
        for e, k in others:
            h_copy(i, e, k).wait_send()
    for s in range(halves):
        for e, k in targets:
            p_copy(s, e, k).wait_send()


def level(moment):
    cosine = jnp.cos((moment / STEPS + 0.008) / 1.008 * math.pi / 2.0)
    return cosine * cosine


def hand_out(state_ref, pred_ref, new_state_ref, new_pred_ref, sems):
    first = pltpu.make_async_copy(state_ref, new_state_ref, sems.at[0])
    second = pltpu.make_async_copy(pred_ref, new_pred_ref, sems.at[1])
    first.start()
    second.start()
    first.wait()
    second.wait()


def per_device(
    sizes, state, prev_pred, ancestors, timestep, w_in, w_time, w_qkv, w_attn_out, w_up, w_down, w_out
):
    ndom, nrow = sizes
    _, rows, width = state.shape
    d, ch = w_out.shape
    cols, height, head = width // ch, rows * nrow, d // HEADS
    ff = w_up.shape[2]
    half = d // 2
    rates = np.exp(-math.log(10000.0) * np.arange(half) / half).astype(np.float32)
    cos_r, sin_r = rope_tables(cols, head, LANES)
    cos_c, sin_c = rope_tables(height, head, LANES)
    tables = jnp.asarray(
        np.concatenate(
            [
                cos_r, sin_r, np.repeat(cos_c, 8, axis=0), np.repeat(sin_c, 8, axis=0),
                np.tile(rates[None], (8, 1)),
            ]
        )
    )
    perm = jnp.asarray(halves_first(d, head).astype(jnp.bfloat16))
    mine = cols // nrow
    wide = min(8, mine)
    pair = max(p for p in range(1, ndom + 1) if ndom % p == 0 and p * p <= ndom and mine % (p * wide) == 0)
    teams, held = ndom // pair, mine // pair
    flat = -(-wide * ch // LANES) * LANES
    halves, steps = held // wide, max(rows // 2, 1)
    cfg = (ndom, nrow, rows, cols, ch, d, head, height, wide, flat, pair)
    vmem = pl.BlockSpec(memory_space=pltpu.VMEM)
    hbm = pl.BlockSpec(memory_space=pl.ANY)
    whole = jax.ShapeDtypeStruct((1, rows, width), BF16)
    dma = pltpu.SemaphoreType.DMA
    stepped, predicted = pl.pallas_call(
        functools.partial(kernel, cfg),
        out_shape=(pltpu.VMEM((1, rows, width), BF16),) * 2,
        in_specs=[hbm] * 13,
        out_specs=(vmem, vmem),
        scratch_shapes=[
            pltpu.SMEM(ancestors.shape, jnp.int32),
            pltpu.SMEM(timestep.shape, jnp.int32),
            pltpu.VMEM(state.shape, BF16),
            pltpu.VMEM(state.shape, BF16),
            pltpu.VMEM(tables.shape, F32),
            pltpu.VMEM(perm.shape, BF16),
            pltpu.VMEM(w_in.shape, BF16),
            pltpu.VMEM(w_time.shape, BF16),
            pltpu.VMEM((ch, d), BF16),
            pltpu.VMEM((2, d, 3 * d), BF16),
            pltpu.VMEM((2, d, d), BF16),
            pltpu.VMEM((2, d, ff), BF16),
            pltpu.VMEM((2, ff, d), BF16),
            pltpu.VMEM((rows * (cols + 8), LANES), F32),
            pltpu.VMEM((rows * (cols + 8), LANES), F32),
            pltpu.VMEM((nrow, pair, rows, held, d), BF16),
            pltpu.VMEM((pair, nrow, rows, held, d), BF16),
            *[pltpu.VMEM((pair, nrow, rows, held, d), F32)] * 3,
            pltpu.VMEM((pair * height * wide, LANES), F32),
            pltpu.VMEM((pair, height, flat), F32),
            pltpu.VMEM((halves, ndom, nrow, rows, flat), BF16),
            pltpu.VMEM((halves, teams, nrow, pair, rows, flat), BF16),
            pltpu.VMEM((pair, rows, width), BF16),
            pltpu.VMEM((teams, rows, width), BF16),
            pltpu.VMEM((teams, rows, width), BF16),
            dma((9,)),
            dma((2, 4)),
            dma,
            dma((pair,)),
            dma((pair,)),
            dma((teams,)),
            dma((teams,)),
            dma((steps, pair, nrow)),
            dma((steps, pair, nrow)),
            dma((halves, ndom, nrow)),
            dma((halves, ndom, nrow)),
        ],
        compiler_params=pltpu.CompilerParams(
            collective_id=0, has_side_effects=True, vmem_limit_bytes=56 * 1024 * 1024,
        ),
    )(
        ancestors, timestep, state, prev_pred, tables, perm, w_in, w_time,
        w_qkv, w_attn_out, w_up, w_down, w_out.T,
    )
    return pl.pallas_call(
        hand_out,
        out_shape=(whole, whole),
        in_specs=[vmem, vmem],
        out_specs=(hbm, hbm),
        scratch_shapes=[dma((2,))],
        compiler_params=pltpu.CompilerParams(vmem_limit_bytes=4 * 1024 * 1024),
    )(stepped, predicted)


def solution(mesh):
    part = P(("group", "dom"), "row", None)
    in_specs = (part, part, P("group"), P("group")) + (P(),) * 7
    return jax.shard_map(
        functools.partial(per_device, (mesh.shape["dom"], mesh.shape["row"])),
        mesh=mesh, in_specs=in_specs, out_specs=(part, part), check_vma=False,
    )
```

```python
import functools
import math

import jax
import jax.numpy as jnp
import numpy as np
from jax import lax
from jax.experimental import pallas as pl
from jax.experimental.pallas import tpu as pltpu
from jax.sharding import PartitionSpec as P

HEADS = 8
STEPS = 1000
STRIDE = 20
LANES = 128
MESH = pl.DeviceIdType.MESH
F32 = jnp.float32
BF16 = jnp.bfloat16


def unit(v):
    return lax.rsqrt(jnp.mean(v * v, axis=-1, keepdims=True) + 1e-06)


def rms(v):
    return v * unit(v)


def mm(a, b):
    return jnp.dot(a, b, preferred_element_type=F32)


def mm_nt(a, b):
    return lax.dot_general(a, b, (((1,), (1,)), ((), ())), preferred_element_type=F32)


def rope_tables(length, head, lanes):
    half = head // 2
    rates = np.exp(-math.log(10000.0) * np.arange(half) / half)
    angles = np.tile(np.arange(length)[:, None] * rates[None, :], (1, lanes // half))
    return np.cos(angles).astype(np.float32), np.sin(angles).astype(np.float32)


def halves_first(d, head):
    half = head // 2
    new = np.arange(d)
    old = (new % (d // 2)) // half * head + new // (d // 2) * half + new % half
    return (np.arange(d)[:, None] == old[None, :]).astype(np.float32)


def rotated(v, by, cos, sin, scale=1.0):
    a, c = v[:, : v.shape[1] // 2], v[:, v.shape[1] // 2 :]
    inv = lax.rsqrt(jnp.mean(v * v, axis=-1, keepdims=True) * (by * by) + 1e-06) * (by * scale)
    return jnp.concatenate([(a * cos - c * sin) * inv, (a * sin + c * cos) * inv], axis=1)


def attention(q, k, v, mask, head):
    n, d = q.shape
    lane = lax.broadcasted_iota(jnp.int32, (1, LANES), 1)
    wide_lane = lax.broadcasted_iota(jnp.int32, (1, d), 1) % (d // 2)
    per = LANES // head
    outs = []
    for part in range(len(v)):
        keys, vals = [], []
        for h in range(per):
            pick = jnp.where(lane // head == h, 1.0, 0.0).astype(BF16)
            pick_key = jnp.where(wide_lane // (head // 2) == part * per + h, 1.0, 0.0).astype(BF16)
            keys.append(k * pick_key)
            vals.append(
                jnp.concatenate([v[part] * pick, jnp.broadcast_to(pick, (n, LANES))], axis=1)
            )
        scores = mm_nt(q, jnp.concatenate(keys, axis=0))
        weights = jnp.exp2(scores.astype(BF16))
        if mask is not None:
            weights = weights * mask
        both = mm(weights, jnp.concatenate(vals, axis=0))
        outs.append(both[:, :LANES] / both[:, LANES:])
    return jnp.concatenate(outs, axis=1).astype(BF16)


def mlp(h, w_up, w_down):
    x = mm(rms(h).astype(BF16), w_up).astype(BF16)
    root = math.sqrt(2.0 / math.pi)
    inner = x * (root + (root * 0.044715) * (x * x))
    gated = x + x * jnp.tanh(inner)
    return (h + 0.5 * mm(gated, w_down)).astype(BF16)


def kernel(
    cfg,
    anc_hbm, time_hbm, state_hbm, prev_hbm, tab_hbm, perm_hbm, w_in_hbm, w_time_hbm,
    w_qkv_hbm, w_attn_hbm, w_up_hbm, w_down_hbm, w_out_hbm,
    state_out, pred_out,
    anc_ref, time_ref, state_ref, prev_ref, tab_ref, perm_ref, w_in_ref, w_time_ref, w_out_ref,
    w_qkv, w_attn, w_up, w_down,
    xs, xp, h1, hcol, q2, k2, v2, ptok, flats, sel, fin, spair, ssel, sfin,
    in_sem, w_sem, own_sem, sa_send, sa_recv, sb_send, sb_recv, h_send, h_recv, p_send, p_recv,
):
    ndom, nrow, rows, cols, ch, d, head, height, wide, flat, pair = cfg
    dom, row = lax.axis_index("dom"), lax.axis_index("row")
    mine = cols // nrow
    group = LANES // math.gcd(ch, LANES)
    glanes = group * ch
    held = mine // pair
    halves = held // wide
    scale = math.log2(math.e) / math.sqrt(head)
    teams = ndom // pair
    team, seat = lax.div(dom, pair), lax.rem(dom, pair)

    def fetch(i, src, dst):
        copy = pltpu.make_async_copy(src, dst, in_sem.at[i])
        copy.start()
        return copy

    got_state = [fetch(0, state_hbm, state_ref), fetch(1, prev_hbm, prev_ref)]
    got_time = [
        fetch(2, time_hbm, time_ref), fetch(3, tab_hbm, tab_ref), fetch(4, w_time_hbm, w_time_ref),
        fetch(5, w_in_hbm, w_in_ref), fetch(8, perm_hbm, perm_ref),
    ]

    pairs = ((w_qkv_hbm, w_qkv), (w_attn_hbm, w_attn), (w_up_hbm, w_up), (w_down_hbm, w_down))

    def load(b, i):
        src, dst = pairs[i]
        copy = pltpu.make_async_copy(src.at[b], dst.at[b], w_sem.at[b, i])
        copy.start()
        return copy

    got_time.append(load(0, 0))
    barrier = pltpu.get_barrier_semaphore()

    def greet(i, carry):
        pl.semaphore_signal(
            barrier,
            inc=1,
            device_id={"dom": lax.rem(dom + lax.div(i, nrow), ndom), "row": lax.rem(row + lax.rem(i, nrow), nrow)},
            device_id_type=MESH,
        )
        return carry

    lax.fori_loop(1, ndom * nrow, greet, 0, unroll=ndom * nrow <= 16)
    loads = [load(0, i) for i in range(1, 4)]
    got_late = [load(1, i) for i in range(4)]
    got_late += [fetch(6, anc_hbm, anc_ref), fetch(7, w_out_hbm, w_out_ref)]
    for copy in got_state + got_time:
        copy.wait()
    own = pltpu.make_async_copy(state_ref.at[0], spair.at[seat], own_sem)
    own.start()

    pitch = xs.shape[0] // rows
    lane = lax.broadcasted_iota(jnp.int32, (rows, LANES), 1)

    def split(c, carry):
        base = pl.multiple_of(c * glanes, LANES)
        for ref, out in ((state_ref, xs), (prev_ref, xp)):
            tiles = [
                ref[0, :, pl.ds(pl.multiple_of(base + j * LANES, LANES), LANES)].astype(F32)
                for j in range(glanes // LANES)
            ]
            for t in range(group):
                j, off = divmod(t * ch, LANES)
                v = pltpu.roll(tiles[j], LANES - off, 1) if off else tiles[j]
                if off + ch > LANES:
                    v = jnp.where(lane < LANES - off, v, pltpu.roll(tiles[j + 1], LANES - off, 1))
                out[pl.ds(c * group + t, rows, stride=pitch), :] = v
        return carry

    lax.fori_loop(0, cols // group, split, 0, unroll=True)

    moment = time_ref[0].astype(F32)
    half = d // 2
    times = jnp.broadcast_to(moment, (1, LANES))
    now, nxt = level(times), level(times - STRIDE)
    c1, c2 = jnp.sqrt(now), jnp.sqrt(nxt)
    c3 = jnp.sqrt(1.0 - nxt) / jnp.sqrt(1.0 - now)
    angles = tab_ref[2 * cols + 16 * height :, :] * moment
    emb = jnp.concatenate([jnp.sin(angles), jnp.cos(angles)], axis=1)
    temb = jnp.dot(
        emb, w_time_ref[...].astype(F32),
        precision=lax.Precision.HIGHEST, preferred_element_type=F32,
    )[0:1]
    w_in = w_in_ref[...].astype(F32)
    gap = jnp.zeros((LANES - ch, d), F32)
    w_in = jnp.concatenate([w_in[:ch], gap, w_in[ch:], gap], axis=0).astype(BF16)

    def halve(b):
        for i in range(2):
            at = slice(i * d, (i + 1) * d)
            w_qkv[b, :, at] = mm(w_qkv[b, :, at], perm_ref[...]).astype(BF16)

    halve(0)
    for copy in loads:
        copy.wait()
    cos_r, sin_r = tab_ref[0:cols], tab_ref[cols : 2 * cols]
    step_rows = 2 if rows % 2 == 0 else 1

    others = [(e, k) for e in range(pair - 1, -1, -1) for k in range(nrow - 1, -1, -1) if (e, k) != (0, 0)]

    def h_copy(i, e, k):
        peer, place = lax.rem(row + k, nrow), lax.rem(seat + e, pair)
        span = pl.ds(i * step_rows, step_rows)
        return pltpu.make_async_remote_copy(
            src_ref=h1.at[peer, place, span],
            dst_ref=hcol.at[seat, row, span],
            send_sem=h_send.at[i, e, k],
            recv_sem=h_recv.at[i, e, k],
            device_id={"dom": team * pair + place, "row": peer},
            device_id_type=MESH,
        )

    def state_pair(e):
        return pltpu.make_async_remote_copy(
            src_ref=state_ref.at[0],
            dst_ref=spair.at[seat],
            send_sem=sa_send.at[e],
            recv_sem=sa_recv.at[e],
            device_id={"dom": team * pair + lax.rem(seat + e, pair)},
            device_id_type=MESH,
        )

    def state_team(e):
        there = lax.rem(team + e, teams)
        return pltpu.make_async_remote_copy(
            src_ref=ssel.at[there],
            dst_ref=sfin.at[team],
            send_sem=sb_send.at[e],
            recv_sem=sb_recv.at[e],
            device_id={"dom": there * pair + seat},
            device_id_type=MESH,
        )

    def pick(there):
        return jnp.clip(anc_ref[there] - team * pair, 0, pair - 1)

    def front(i):
        x = jnp.concatenate(
            [
                jnp.concatenate([v[r * pitch : r * pitch + cols, :].astype(BF16) for v in (xs, xp)], axis=1)
                for r in range(i * step_rows, (i + 1) * step_rows)
            ],
            axis=0,
        )
        h = mm(x, w_in) + temb
        low = h.astype(BF16)
        h = low.astype(F32)
        by = unit(h)
        qkv = mm(low, w_qkv[0])
        cos = jnp.concatenate([cos_r] * step_rows, axis=0)
        sin = jnp.concatenate([sin_r] * step_rows, axis=0)
        q = rotated(qkv[:, :d], by, cos, sin, scale).astype(BF16)
        k = rotated(qkv[:, d : 2 * d], by, cos, sin).astype(BF16)
        v = (qkv[:, 2 * d :] * by).astype(BF16)
        v = [v[:, p * LANES : (p + 1) * LANES] for p in range(d // LANES)]
        return h, q, k, v

    def middle(h, q, k, v):
        mixed = []
        for r in range(step_rows):
            a, b = r * cols, (r + 1) * cols
            mixed.append(attention(q[a:b], k[a:b], [x[a:b] for x in v], None, head))
        o = jnp.concatenate(mixed, axis=0)
        return (h + mm(o, w_attn[0])).astype(BF16).astype(F32)

    def back(i, h):
        h = mlp(h, w_up[0], w_down[0]).reshape(step_rows, cols, d)
        span = slice(i * step_rows, (i + 1) * step_rows)
        for g in range(nrow * pair):
            h1[g // pair, g % pair, span] = h[:, g * held : (g + 1) * held, :]

    def send(i):
        for e, k in others:
            h_copy(i, e, k).start()

    def enter():
        pl.semaphore_wait(barrier, ndom * nrow - 1)
        for e in range(1, pair):
            state_pair(e).start()

    made = front(0)
    enter()
    for i in range(rows // step_rows):
        h = middle(*made)
        if i + 1 < rows // step_rows:
            made = front(i + 1)
        back(i, h)
        send(i)

    for copy in got_late:
        copy.wait()

    hcol[seat, row] = h1[row, seat]
    halve(1)

    cos_c = tab_ref[2 * cols : 2 * cols + 8 * height].reshape(height, 8, LANES)
    sin_c = tab_ref[2 * cols + 8 * height : 2 * cols + 16 * height].reshape(height, 8, LANES)
    cos_c = jnp.concatenate([cos_c] * (held // 8), axis=1).reshape(nrow, rows, held, LANES)
    sin_c = jnp.concatenate([sin_c] * (held // 8), axis=1).reshape(nrow, rows, held, LANES)
    sub = height * wide
    n1 = pair * sub
    n2 = pair * nrow * step_rows * held
    per = LANES // head
    qi = lax.broadcasted_iota(jnp.int32, (sub, per * sub), 0)
    ki = lax.broadcasted_iota(jnp.int32, (sub, per * sub), 1)
    mask = jnp.where(qi % wide == ki % wide, 1.0, 0.0).astype(BF16)
    hlane = lax.broadcasted_iota(jnp.int32, (height // (2 if nrow % 2 == 0 else 1), LANES), 1)

    def project(i):
        span = slice(i * step_rows, (i + 1) * step_rows)
        low = hcol[:, :, span].reshape(n2, d)
        by = unit(low.astype(F32))
        qkv = mm(low, w_qkv[1])
        cos = jnp.concatenate([cos_c[:, span].reshape(n2 // pair, LANES)] * pair, axis=0)
        sin = jnp.concatenate([sin_c[:, span].reshape(n2 // pair, LANES)] * pair, axis=0)
        shape = (pair, nrow, step_rows, held, d)
        q2[:, :, span] = rotated(qkv[:, :d], by, cos, sin, scale).reshape(shape)
        k2[:, :, span] = rotated(qkv[:, d : 2 * d], by, cos, sin).reshape(shape)
        v2[:, :, span] = (qkv[:, 2 * d :] * by).reshape(shape)

    for i in range(rows // step_rows):
        for e, k in others:
            h_copy(i, e, k).wait_recv()
        project(i)
        if i == 0:
            own.wait()
            for e in range(1, pair):
                state_pair(e).wait_recv()
            for e in range(1, teams):
                there = lax.rem(team + e, teams)
                ssel[there] = spair[pick(there * pair + seat)]
                state_team(e).start()
            sfin[team] = spair[pick(dom)]

    def second(s):
        span = slice(s * wide, (s + 1) * wide)
        mixed = []
        for p in range(pair):
            q, k, v = (x[p, :, :, span, :].reshape(sub, d).astype(BF16) for x in (q2, k2, v2))
            v = [v[:, t * LANES : (t + 1) * LANES] for t in range(d // LANES)]
            mixed.append(attention(q, k, v, mask, head))
        o = jnp.concatenate(mixed, axis=0)
        h = hcol[...].astype(F32)[:, :, :, span, :].reshape(n1, d)
        return (h + mm(o, w_attn[1])).astype(BF16).astype(F32)

    cuts = 2 if nrow % 2 == 0 else 1
    part, peers = height // cuts, nrow // cuts
    ends = [0] + [(s + 1) * wide * ch // LANES for s in range(halves - 1)] + [flat // LANES]

    def shared(h, u):
        h = h.reshape(pair, height * wide, d)[:, u * part * wide : (u + 1) * part * wide]
        return h.reshape(pair * part * wide, d)

    def finish(s, u, low):
        out = mm_nt(low, w_out_ref[...]) * unit(low.astype(F32))

        def base(s, p):
            return s * n1 + (p * height + u * part) * wide

        for p in range(pair):
            ptok[base(s, p) : base(s, p) + part * wide, 0:ch] = out[p * part * wide : (p + 1) * part * wide]
        for p in range(pair):
            toks = {}
            for j in range(ends[s], ends[s + 1]):
                acc = None
                for t in range(j * LANES // ch, min((j * LANES + LANES - 1) // ch, (s + 1) * wide - 1) + 1):
                    if t not in toks:
                        toks[t] = ptok[pl.ds(base(t // wide, p) + t % wide, part, stride=wide), :]
                    at = t * ch - j * LANES
                    x = pltpu.roll(toks[t], at % LANES, 1) if at % LANES else toks[t]
                    acc = x if acc is None else jnp.where(hlane >= at, x, acc)
                flats[p, u * part : (u + 1) * part, j * LANES : (j + 1) * LANES] = acc
        span = slice(ends[s] * LANES, ends[s + 1] * LANES)
        for there in range(ndom):
            want = pick(there)
            for r in range(u * peers, (u + 1) * peers):
                sel[there, r, :, span] = flats[want, r * rows : (r + 1) * rows, span].astype(BF16)

    def p_copy(s, e, peer, sent, got):
        there = lax.rem(dom + e, ndom)
        span = pl.ds(ends[s] * LANES, (ends[s + 1] - ends[s]) * LANES)
        return pltpu.make_async_remote_copy(
            src_ref=sel.at[there, peer, :, span],
            dst_ref=fin.at[team, row, seat, :, span],
            send_sem=p_send.at[s, e, sent],
            recv_sem=p_recv.at[s, e, got],
            device_id={"dom": there, "row": peer},
            device_id_type=MESH,
        )

    def p_far(s, e, r):
        return p_copy(s, e, r, r, row)

    def p_near(s, k):
        return p_copy(s, 0, lax.rem(row + k, nrow), k, k)

    def p_all(s):
        return [p_copy(s, e, r, r, r) for e in range(1, ndom) for r in range(nrow)] + [
            p_near(s, k) for k in range(1, nrow)
        ]

    upper = lax.div(dom, max(ndom // 2, 1))
    later = lax.div(upper + 1, 2)

    def far_first(j):
        return later * j + (1 - later) * (ndom - j)

    def post(s, u):
        for j in range(1, ndom):
            for r in range(u * peers, (u + 1) * peers):
                p_far(s, far_first(j), r).start()
        if u == cuts - 1:
            span = slice(ends[s] * LANES, ends[s + 1] * LANES)
            for k in range(1, nrow):
                p_near(s, k).start()
            fin[team, row, seat, :, span] = sel[dom, row, :, span]

    for s in range(halves):
        h = second(s)
        if s < halves - 1:
            low = mlp(h, w_up[1], w_down[1])
        for u in range(cuts):
            if s == halves - 1:
                finish(s, u, mlp(shared(h, u), w_up[1], w_down[1]))
            else:
                finish(s, u, shared(low, u))
            post(s, u)
    for e in range(1, teams):
        state_team(e).wait_recv()
    home = lax.div(anc_ref[dom], pair)

    for s in range(halves):
        for copy in p_all(s):
            copy.wait_recv()

    size = held * ch
    count = flat // LANES

    def piece(q, offset):
        tile, rem = divmod(offset, LANES)

        def load(j):
            x = fin[home, q // pair, q % pair, :, j * LANES : (j + 1) * LANES].astype(F32)
            return pltpu.roll(x, LANES - rem, 1) if rem else x

        low = load(tile) if tile >= 0 else None
        if not rem or tile + 1 >= count:
            return low
        high = load(tile + 1)
        return high if low is None else jnp.where(lane < LANES - rem, low, high)

    for j in range(cols * ch // LANES):
        start = j * LANES
        acc = None
        for q in range(start // size, (start + LANES - 1) // size + 1):
            x = piece(q, start - q * size)
            acc = x if acc is None else jnp.where(lane >= q * size - start, x, acc)
        acc = acc.astype(BF16)
        pred_out[0, :, start : start + LANES] = acc
        pred = acc.astype(F32)
        old = sfin[home, :, start : start + LANES].astype(F32)
        state_out[0, :, start : start + LANES] = (c2 * pred + c3 * (old - c1 * pred)).astype(BF16)

    for e in range(1, pair):
        state_pair(e).wait_send()
    for e in range(1, teams):
        state_team(e).wait_send()
    for i in range(rows // step_rows):
        for e, k in others:
            h_copy(i, e, k).wait_send()
    for s in range(halves):
        for copy in p_all(s):
            copy.wait_send()


def level(moment):
    cosine = jnp.cos((moment / STEPS + 0.008) / 1.008 * math.pi / 2.0)
    return cosine * cosine


def hand_out(state_ref, pred_ref, new_state_ref, new_pred_ref, sems):
    first = pltpu.make_async_copy(state_ref, new_state_ref, sems.at[0])
    second = pltpu.make_async_copy(pred_ref, new_pred_ref, sems.at[1])
    first.start()
    second.start()
    first.wait()
    second.wait()


def per_device(
    sizes, state, prev_pred, ancestors, timestep, w_in, w_time, w_qkv, w_attn_out, w_up, w_down, w_out
):
    ndom, nrow = sizes
    _, rows, width = state.shape
    d, ch = w_out.shape
    cols, height, head = width // ch, rows * nrow, d // HEADS
    ff = w_up.shape[2]
    half = d // 2
    rates = np.exp(-math.log(10000.0) * np.arange(half) / half).astype(np.float32)
    cos_r, sin_r = rope_tables(cols, head, LANES)
    cos_c, sin_c = rope_tables(height, head, LANES)
    tables = jnp.asarray(
        np.concatenate(
            [
                cos_r, sin_r, np.repeat(cos_c, 8, axis=0), np.repeat(sin_c, 8, axis=0),
                np.tile(rates[None], (8, 1)),
            ]
        )
    )
    perm = jnp.asarray(halves_first(d, head).astype(jnp.bfloat16))
    mine = cols // nrow
    wide = min(8, mine)
    pair = max(p for p in range(1, ndom + 1) if ndom % p == 0 and p * p <= ndom and mine % (p * wide) == 0)
    teams, held = ndom // pair, mine // pair
    flat = -(-held * ch // LANES) * LANES
    halves, steps = held // wide, max(rows // 2, 1)
    cfg = (ndom, nrow, rows, cols, ch, d, head, height, wide, flat, pair)
    vmem = pl.BlockSpec(memory_space=pltpu.VMEM)
    hbm = pl.BlockSpec(memory_space=pl.ANY)
    whole = jax.ShapeDtypeStruct((1, rows, width), BF16)
    dma = pltpu.SemaphoreType.DMA
    stepped, predicted = pl.pallas_call(
        functools.partial(kernel, cfg),
        out_shape=(pltpu.VMEM((1, rows, width), BF16),) * 2,
        in_specs=[hbm] * 13,
        out_specs=(vmem, vmem),
        scratch_shapes=[
            pltpu.SMEM(ancestors.shape, jnp.int32),
            pltpu.SMEM(timestep.shape, jnp.int32),
            pltpu.VMEM(state.shape, BF16),
            pltpu.VMEM(state.shape, BF16),
            pltpu.VMEM(tables.shape, F32),
            pltpu.VMEM(perm.shape, BF16),
            pltpu.VMEM(w_in.shape, BF16),
            pltpu.VMEM(w_time.shape, BF16),
            pltpu.VMEM((ch, d), BF16),
            pltpu.VMEM((2, d, 3 * d), BF16),
            pltpu.VMEM((2, d, d), BF16),
            pltpu.VMEM((2, d, ff), BF16),
            pltpu.VMEM((2, ff, d), BF16),
            pltpu.VMEM((rows * (cols + 8), LANES), F32),
            pltpu.VMEM((rows * (cols + 8), LANES), F32),
            pltpu.VMEM((nrow, pair, rows, held, d), BF16),
            pltpu.VMEM((pair, nrow, rows, held, d), BF16),
            *[pltpu.VMEM((pair, nrow, rows, held, d), F32)] * 3,
            pltpu.VMEM((pair * height * held, LANES), F32),
            pltpu.VMEM((pair, height, flat), F32),
            pltpu.VMEM((ndom, nrow, rows, flat), BF16),
            pltpu.VMEM((teams, nrow, pair, rows, flat), BF16),
            pltpu.VMEM((pair, rows, width), BF16),
            pltpu.VMEM((teams, rows, width), BF16),
            pltpu.VMEM((teams, rows, width), BF16),
            dma((9,)),
            dma((2, 4)),
            dma,
            dma((pair,)),
            dma((pair,)),
            dma((teams,)),
            dma((teams,)),
            dma((steps, pair, nrow)),
            dma((steps, pair, nrow)),
            dma((halves, ndom, nrow)),
            dma((halves, ndom, nrow)),
        ],
        compiler_params=pltpu.CompilerParams(
            collective_id=0, has_side_effects=True, vmem_limit_bytes=56 * 1024 * 1024,
        ),
    )(
        ancestors, timestep, state, prev_pred, tables, perm, w_in, w_time,
        w_qkv, w_attn_out, w_up, w_down, w_out.T,
    )
    return pl.pallas_call(
        hand_out,
        out_shape=(whole, whole),
        in_specs=[vmem, vmem],
        out_specs=(hbm, hbm),
        scratch_shapes=[dma((2,))],
        compiler_params=pltpu.CompilerParams(vmem_limit_bytes=4 * 1024 * 1024),
    )(stepped, predicted)


def solution(mesh):
    part = P(("group", "dom"), "row", None)
    in_specs = (part, part, P("group"), P("group")) + (P(),) * 7
    return jax.shard_map(
        functools.partial(per_device, (mesh.shape["dom"], mesh.shape["row"])),
        mesh=mesh, in_specs=in_specs, out_specs=(part, part), check_vma=False,
    )
```

```python
import functools
import math

import jax
import jax.numpy as jnp
import numpy as np
from jax import lax
from jax.experimental import pallas as pl
from jax.experimental.pallas import tpu as pltpu
from jax.sharding import PartitionSpec as P

HEADS = 8
STEPS = 1000
STRIDE = 20
LANES = 128
MESH = pl.DeviceIdType.MESH
F32 = jnp.float32
BF16 = jnp.bfloat16


def unit(v):
    return lax.rsqrt(jnp.mean(v * v, axis=-1, keepdims=True) + 1e-06)


def rms(v):
    return v * unit(v)


def mm(a, b):
    return jnp.dot(a, b, preferred_element_type=F32)


def mm_nt(a, b):
    return lax.dot_general(a, b, (((1,), (1,)), ((), ())), preferred_element_type=F32)


def rope_tables(length, head, lanes):
    half = head // 2
    rates = np.exp(-math.log(10000.0) * np.arange(half) / half)
    angles = np.tile(np.arange(length)[:, None] * rates[None, :], (1, lanes // half))
    return np.cos(angles).astype(np.float32), np.sin(angles).astype(np.float32)


def halves_first(d, head):
    half = head // 2
    new = np.arange(d)
    old = (new % (d // 2)) // half * head + new // (d // 2) * half + new % half
    return (np.arange(d)[:, None] == old[None, :]).astype(np.float32)


def rotated(v, by, cos, sin, scale=1.0):
    a, c = v[:, : v.shape[1] // 2], v[:, v.shape[1] // 2 :]
    inv = lax.rsqrt(jnp.mean(v * v, axis=-1, keepdims=True) * (by * by) + 1e-06) * (by * scale)
    return jnp.concatenate([(a * cos - c * sin) * inv, (a * sin + c * cos) * inv], axis=1)


def attention(q, k, v, mask, head):
    n, d = q.shape
    lane = lax.broadcasted_iota(jnp.int32, (1, LANES), 1)
    wide_lane = lax.broadcasted_iota(jnp.int32, (1, d), 1) % (d // 2)
    per = LANES // head
    outs = []
    for part in range(len(v)):
        keys, vals = [], []
        for h in range(per):
            pick = jnp.where(lane // head == h, 1.0, 0.0).astype(BF16)
            pick_key = jnp.where(wide_lane // (head // 2) == part * per + h, 1.0, 0.0).astype(BF16)
            keys.append(k * pick_key)
            vals.append(
                jnp.concatenate([v[part] * pick, jnp.broadcast_to(pick, (n, LANES))], axis=1)
            )
        scores = mm_nt(q, jnp.concatenate(keys, axis=0))
        weights = jnp.exp2(scores.astype(BF16))
        if mask is not None:
            weights = weights * mask
        both = mm(weights, jnp.concatenate(vals, axis=0))
        outs.append(both[:, :LANES] / both[:, LANES:])
    return jnp.concatenate(outs, axis=1).astype(BF16)


def mlp(h, w_up, w_down):
    x = mm(rms(h).astype(BF16), w_up).astype(BF16)
    root = math.sqrt(2.0 / math.pi)
    inner = x * (root + (root * 0.044715) * (x * x))
    gated = x + x * jnp.tanh(inner)
    return (h + 0.5 * mm(gated, w_down)).astype(BF16)


def kernel(
    cfg,
    anc_hbm, time_hbm, state_hbm, prev_hbm, tab_hbm, perm_hbm, w_in_hbm, w_time_hbm,
    w_qkv_hbm, w_attn_hbm, w_up_hbm, w_down_hbm, w_out_hbm,
    state_out, pred_out,
    anc_ref, time_ref, state_ref, prev_ref, tab_ref, perm_ref, w_in_ref, w_time_ref, w_out_ref,
    w_qkv, w_attn, w_up, w_down,
    xs, xp, h1, hcol, q2, k2, v2, ptok, flats, sel, fin, spair, ssel, sfin,
    in_sem, w_sem, own_sem, sa_send, sa_recv, sb_send, sb_recv, h_send, h_recv, p_send, p_recv,
):
    ndom, nrow, rows, cols, ch, d, head, height, wide, flat, pair = cfg
    dom, row = lax.axis_index("dom"), lax.axis_index("row")
    mine = cols // nrow
    group = LANES // math.gcd(ch, LANES)
    glanes = group * ch
    held = mine // pair
    halves = held // wide
    scale = math.log2(math.e) / math.sqrt(head)
    teams = ndom // pair
    team, seat = lax.div(dom, pair), lax.rem(dom, pair)

    def fetch(i, src, dst):
        copy = pltpu.make_async_copy(src, dst, in_sem.at[i])
        copy.start()
        return copy

    got_state = [fetch(0, state_hbm, state_ref), fetch(1, prev_hbm, prev_ref)]
    got_time = [
        fetch(2, time_hbm, time_ref), fetch(3, tab_hbm, tab_ref), fetch(4, w_time_hbm, w_time_ref),
        fetch(5, w_in_hbm, w_in_ref), fetch(8, perm_hbm, perm_ref),
    ]

    pairs = ((w_qkv_hbm, w_qkv), (w_attn_hbm, w_attn), (w_up_hbm, w_up), (w_down_hbm, w_down))

    def load(b, i):
        src, dst = pairs[i]
        copy = pltpu.make_async_copy(src.at[b], dst.at[b], w_sem.at[b, i])
        copy.start()
        return copy

    got_time.append(load(0, 0))
    barrier = pltpu.get_barrier_semaphore()

    def greet(i, carry):
        pl.semaphore_signal(
            barrier,
            inc=1,
            device_id={"dom": lax.rem(dom + lax.div(i, nrow), ndom), "row": lax.rem(row + lax.rem(i, nrow), nrow)},
            device_id_type=MESH,
        )
        return carry

    lax.fori_loop(1, ndom * nrow, greet, 0, unroll=ndom * nrow <= 16)
    loads = [load(0, i) for i in range(1, 4)]
    got_late = [load(1, i) for i in range(4)]
    got_late += [fetch(6, anc_hbm, anc_ref), fetch(7, w_out_hbm, w_out_ref)]
    for copy in got_state + got_time:
        copy.wait()
    own = pltpu.make_async_copy(state_ref.at[0], spair.at[seat], own_sem)
    own.start()

    pitch = xs.shape[0] // rows
    lane = lax.broadcasted_iota(jnp.int32, (rows, LANES), 1)

    def split(c, carry):
        base = pl.multiple_of(c * glanes, LANES)
        for ref, out in ((state_ref, xs), (prev_ref, xp)):
            tiles = [
                ref[0, :, pl.ds(pl.multiple_of(base + j * LANES, LANES), LANES)].astype(F32)
                for j in range(glanes // LANES)
            ]
            for t in range(group):
                j, off = divmod(t * ch, LANES)
                v = pltpu.roll(tiles[j], LANES - off, 1) if off else tiles[j]
                if off + ch > LANES:
                    v = jnp.where(lane < LANES - off, v, pltpu.roll(tiles[j + 1], LANES - off, 1))
                out[pl.ds(c * group + t, rows, stride=pitch), :] = v
        return carry

    lax.fori_loop(0, cols // group, split, 0, unroll=True)

    moment = time_ref[0].astype(F32)
    half = d // 2
    times = jnp.broadcast_to(moment, (1, LANES))
    now, nxt = level(times), level(times - STRIDE)
    c1, c2 = jnp.sqrt(now), jnp.sqrt(nxt)
    c3 = jnp.sqrt(1.0 - nxt) / jnp.sqrt(1.0 - now)
    angles = tab_ref[2 * cols + 16 * height :, :] * moment
    emb = jnp.concatenate([jnp.sin(angles), jnp.cos(angles)], axis=1)
    temb = jnp.dot(
        emb, w_time_ref[...].astype(F32),
        precision=lax.Precision.HIGHEST, preferred_element_type=F32,
    )[0:1]
    w_in = w_in_ref[...].astype(F32)
    gap = jnp.zeros((LANES - ch, d), F32)
    w_in = jnp.concatenate([w_in[:ch], gap, w_in[ch:], gap], axis=0).astype(BF16)

    def halve(b):
        for i in range(2):
            at = slice(i * d, (i + 1) * d)
            w_qkv[b, :, at] = mm(w_qkv[b, :, at], perm_ref[...]).astype(BF16)

    halve(0)
    for copy in loads:
        copy.wait()
    cos_r, sin_r = tab_ref[0:cols], tab_ref[cols : 2 * cols]
    step_rows = 2 if rows % 2 == 0 else 1

    others = [(e, k) for e in range(pair - 1, -1, -1) for k in range(nrow - 1, -1, -1) if (e, k) != (0, 0)]

    def h_copy(i, e, k):
        peer, place = lax.rem(row + k, nrow), lax.rem(seat + e, pair)
        span = pl.ds(i * step_rows, step_rows)
        return pltpu.make_async_remote_copy(
            src_ref=h1.at[peer, place, span],
            dst_ref=hcol.at[seat, row, span],
            send_sem=h_send.at[i, e, k],
            recv_sem=h_recv.at[i, e, k],
            device_id={"dom": team * pair + place, "row": peer},
            device_id_type=MESH,
        )

    def state_pair(e):
        return pltpu.make_async_remote_copy(
            src_ref=state_ref.at[0],
            dst_ref=spair.at[seat],
            send_sem=sa_send.at[e],
            recv_sem=sa_recv.at[e],
            device_id={"dom": team * pair + lax.rem(seat + e, pair)},
            device_id_type=MESH,
        )

    def state_team(e):
        there = lax.rem(team + e, teams)
        return pltpu.make_async_remote_copy(
            src_ref=ssel.at[there],
            dst_ref=sfin.at[team],
            send_sem=sb_send.at[e],
            recv_sem=sb_recv.at[e],
            device_id={"dom": there * pair + seat},
            device_id_type=MESH,
        )

    def pick(there):
        return jnp.clip(anc_ref[there] - team * pair, 0, pair - 1)

    def front(i):
        x = jnp.concatenate(
            [
                jnp.concatenate([v[r * pitch : r * pitch + cols, :].astype(BF16) for v in (xs, xp)], axis=1)
                for r in range(i * step_rows, (i + 1) * step_rows)
            ],
            axis=0,
        )
        h = mm(x, w_in) + temb
        low = h.astype(BF16)
        h = low.astype(F32)
        by = unit(h)
        qkv = mm(low, w_qkv[0])
        cos = jnp.concatenate([cos_r] * step_rows, axis=0)
        sin = jnp.concatenate([sin_r] * step_rows, axis=0)
        q = rotated(qkv[:, :d], by, cos, sin, scale).astype(BF16)
        k = rotated(qkv[:, d : 2 * d], by, cos, sin).astype(BF16)
        v = (qkv[:, 2 * d :] * by).astype(BF16)
        v = [v[:, p * LANES : (p + 1) * LANES] for p in range(d // LANES)]
        return h, q, k, v

    def middle(h, q, k, v):
        mixed = []
        for r in range(step_rows):
            a, b = r * cols, (r + 1) * cols
            mixed.append(attention(q[a:b], k[a:b], [x[a:b] for x in v], None, head))
        o = jnp.concatenate(mixed, axis=0)
        return (h + mm(o, w_attn[0])).astype(BF16).astype(F32)

    def back(i, h):
        h = mlp(h, w_up[0], w_down[0]).reshape(step_rows, cols, d)
        span = slice(i * step_rows, (i + 1) * step_rows)
        for g in range(nrow * pair):
            h1[g // pair, g % pair, span] = h[:, g * held : (g + 1) * held, :]

    def send(i):
        for e, k in others:
            h_copy(i, e, k).start()

    def enter():
        pl.semaphore_wait(barrier, ndom * nrow - 1)
        for e in range(1, pair):
            state_pair(e).start()

    made = front(0)
    enter()
    for i in range(rows // step_rows):
        h = middle(*made)
        if i + 1 < rows // step_rows:
            made = front(i + 1)
        back(i, h)
        send(i)

    for copy in got_late:
        copy.wait()

    hcol[seat, row] = h1[row, seat]
    halve(1)

    cos_c = tab_ref[2 * cols : 2 * cols + 8 * height].reshape(height, 8, LANES)
    sin_c = tab_ref[2 * cols + 8 * height : 2 * cols + 16 * height].reshape(height, 8, LANES)
    cos_c = jnp.concatenate([cos_c] * (held // 8), axis=1).reshape(nrow, rows, held, LANES)
    sin_c = jnp.concatenate([sin_c] * (held // 8), axis=1).reshape(nrow, rows, held, LANES)
    sub = height * wide
    n1 = pair * sub
    n2 = pair * nrow * step_rows * held
    per = LANES // head
    qi = lax.broadcasted_iota(jnp.int32, (sub, per * sub), 0)
    ki = lax.broadcasted_iota(jnp.int32, (sub, per * sub), 1)
    mask = jnp.where(qi % wide == ki % wide, 1.0, 0.0).astype(BF16)
    hlane = lax.broadcasted_iota(jnp.int32, (height // (2 if nrow % 2 == 0 else 1), LANES), 1)

    def project(i):
        span = slice(i * step_rows, (i + 1) * step_rows)
        low = hcol[:, :, span].reshape(n2, d)
        by = unit(low.astype(F32))
        qkv = mm(low, w_qkv[1])
        cos = jnp.concatenate([cos_c[:, span].reshape(n2 // pair, LANES)] * pair, axis=0)
        sin = jnp.concatenate([sin_c[:, span].reshape(n2 // pair, LANES)] * pair, axis=0)
        shape = (pair, nrow, step_rows, held, d)
        q2[:, :, span] = rotated(qkv[:, :d], by, cos, sin, scale).reshape(shape)
        k2[:, :, span] = rotated(qkv[:, d : 2 * d], by, cos, sin).reshape(shape)
        v2[:, :, span] = (qkv[:, 2 * d :] * by).reshape(shape)

    for i in range(rows // step_rows):
        for e, k in others:
            h_copy(i, e, k).wait_recv()
        if i == 0:
            own.wait()
            for e in range(1, pair):
                state_pair(e).wait_recv()
            for e in range(1, teams):
                there = lax.rem(team + e, teams)
                ssel[there] = spair[pick(there * pair + seat)]
                state_team(e).start()
            sfin[team] = spair[pick(dom)]
        project(i)

    def second(s):
        span = slice(s * wide, (s + 1) * wide)
        mixed = []
        for p in range(pair):
            q, k, v = (x[p, :, :, span, :].reshape(sub, d).astype(BF16) for x in (q2, k2, v2))
            v = [v[:, t * LANES : (t + 1) * LANES] for t in range(d // LANES)]
            mixed.append(attention(q, k, v, mask, head))
        o = jnp.concatenate(mixed, axis=0)
        h = hcol[...].astype(F32)[:, :, :, span, :].reshape(n1, d)
        return (h + mm(o, w_attn[1])).astype(BF16).astype(F32)

    cuts = 2 if nrow % 2 == 0 else 1
    part, peers = height // cuts, nrow // cuts
    ends = [0] + [(s + 1) * wide * ch // LANES for s in range(halves - 1)] + [flat // LANES]

    def shared(h, u):
        h = h.reshape(pair, height * wide, d)[:, u * part * wide : (u + 1) * part * wide]
        return h.reshape(pair * part * wide, d)

    def finish(s, u, low):
        out = mm_nt(low, w_out_ref[...]) * unit(low.astype(F32))

        def base(s, p):
            return s * n1 + (p * height + u * part) * wide

        for p in range(pair):
            ptok[base(s, p) : base(s, p) + part * wide, 0:ch] = out[p * part * wide : (p + 1) * part * wide]
        for p in range(pair):
            toks = {}
            for j in range(ends[s], ends[s + 1]):
                acc = None
                for t in range(j * LANES // ch, min((j * LANES + LANES - 1) // ch, (s + 1) * wide - 1) + 1):
                    if t not in toks:
                        toks[t] = ptok[pl.ds(base(t // wide, p) + t % wide, part, stride=wide), :]
                    at = t * ch - j * LANES
                    x = pltpu.roll(toks[t], at % LANES, 1) if at % LANES else toks[t]
                    acc = x if acc is None else jnp.where(hlane >= at, x, acc)
                flats[p, u * part : (u + 1) * part, j * LANES : (j + 1) * LANES] = acc
        span = slice(ends[s] * LANES, ends[s + 1] * LANES)
        for there in range(ndom):
            want = pick(there)
            for r in range(u * peers, (u + 1) * peers):
                sel[there, r, :, span] = flats[want, r * rows : (r + 1) * rows, span].astype(BF16)

    def p_copy(s, e, peer, sent, got):
        there = lax.rem(dom + e, ndom)
        span = pl.ds(ends[s] * LANES, (ends[s + 1] - ends[s]) * LANES)
        return pltpu.make_async_remote_copy(
            src_ref=sel.at[there, peer, :, span],
            dst_ref=fin.at[team, row, seat, :, span],
            send_sem=p_send.at[s, e, sent],
            recv_sem=p_recv.at[s, e, got],
            device_id={"dom": there, "row": peer},
            device_id_type=MESH,
        )

    def p_far(s, e, r):
        return p_copy(s, e, r, r, row)

    def p_near(s, k):
        return p_copy(s, 0, lax.rem(row + k, nrow), k, k)

    def p_all(s):
        return [p_copy(s, e, r, r, r) for e in range(1, ndom) for r in range(nrow)] + [
            p_near(s, k) for k in range(1, nrow)
        ]

    upper = lax.div(dom, max(ndom // 2, 1))
    later = lax.div(upper + 1, 2)

    def far_first(j):
        return later * j + (1 - later) * (ndom - j)

    def post(s, u):
        for j in range(1, ndom):
            for r in range(u * peers, (u + 1) * peers):
                p_far(s, far_first(j), r).start()
        if u == cuts - 1:
            span = slice(ends[s] * LANES, ends[s + 1] * LANES)
            for k in range(1, nrow):
                p_near(s, k).start()
            fin[team, row, seat, :, span] = sel[dom, row, :, span]

    for s in range(halves):
        h = second(s)
        if s < halves - 1:
            low = mlp(h, w_up[1], w_down[1])
        for u in range(cuts):
            if s == halves - 1:
                finish(s, u, mlp(shared(h, u), w_up[1], w_down[1]))
            else:
                finish(s, u, shared(low, u))
            post(s, u)
    for e in range(1, teams):
        state_team(e).wait_recv()
    home = lax.div(anc_ref[dom], pair)

    for s in range(halves):
        for copy in p_all(s):
            copy.wait_recv()

    size = held * ch
    count = flat // LANES

    def piece(q, offset):
        tile, rem = divmod(offset, LANES)

        def load(j):
            x = fin[home, q // pair, q % pair, :, j * LANES : (j + 1) * LANES].astype(F32)
            return pltpu.roll(x, LANES - rem, 1) if rem else x

        low = load(tile) if tile >= 0 else None
        if not rem or tile + 1 >= count:
            return low
        high = load(tile + 1)
        return high if low is None else jnp.where(lane < LANES - rem, low, high)

    for j in range(cols * ch // LANES):
        start = j * LANES
        acc = None
        for q in range(start // size, (start + LANES - 1) // size + 1):
            x = piece(q, start - q * size)
            acc = x if acc is None else jnp.where(lane >= q * size - start, x, acc)
        acc = acc.astype(BF16)
        pred_out[0, :, start : start + LANES] = acc
        pred = acc.astype(F32)
        old = sfin[home, :, start : start + LANES].astype(F32)
        state_out[0, :, start : start + LANES] = (c2 * pred + c3 * (old - c1 * pred)).astype(BF16)

    for e in range(1, pair):
        state_pair(e).wait_send()
    for e in range(1, teams):
        state_team(e).wait_send()
    for i in range(rows // step_rows):
        for e, k in others:
            h_copy(i, e, k).wait_send()
    for s in range(halves):
        for copy in p_all(s):
            copy.wait_send()


def level(moment):
    cosine = jnp.cos((moment / STEPS + 0.008) / 1.008 * math.pi / 2.0)
    return cosine * cosine


def hand_out(state_ref, pred_ref, new_state_ref, new_pred_ref, sems):
    first = pltpu.make_async_copy(state_ref, new_state_ref, sems.at[0])
    second = pltpu.make_async_copy(pred_ref, new_pred_ref, sems.at[1])
    first.start()
    second.start()
    first.wait()
    second.wait()


def per_device(
    sizes, state, prev_pred, ancestors, timestep, w_in, w_time, w_qkv, w_attn_out, w_up, w_down, w_out
):
    ndom, nrow = sizes
    _, rows, width = state.shape
    d, ch = w_out.shape
    cols, height, head = width // ch, rows * nrow, d // HEADS
    ff = w_up.shape[2]
    half = d // 2
    rates = np.exp(-math.log(10000.0) * np.arange(half) / half).astype(np.float32)
    cos_r, sin_r = rope_tables(cols, head, LANES)
    cos_c, sin_c = rope_tables(height, head, LANES)
    tables = jnp.asarray(
        np.concatenate(
            [
                cos_r, sin_r, np.repeat(cos_c, 8, axis=0), np.repeat(sin_c, 8, axis=0),
                np.tile(rates[None], (8, 1)),
            ]
        )
    )
    perm = jnp.asarray(halves_first(d, head).astype(jnp.bfloat16))
    mine = cols // nrow
    wide = min(8, mine)
    pair = max(p for p in range(1, ndom + 1) if ndom % p == 0 and p * p <= ndom and mine % (p * wide) == 0)
    teams, held = ndom // pair, mine // pair
    flat = -(-held * ch // LANES) * LANES
    halves, steps = held // wide, max(rows // 2, 1)
    cfg = (ndom, nrow, rows, cols, ch, d, head, height, wide, flat, pair)
    vmem = pl.BlockSpec(memory_space=pltpu.VMEM)
    hbm = pl.BlockSpec(memory_space=pl.ANY)
    whole = jax.ShapeDtypeStruct((1, rows, width), BF16)
    dma = pltpu.SemaphoreType.DMA
    stepped, predicted = pl.pallas_call(
        functools.partial(kernel, cfg),
        out_shape=(pltpu.VMEM((1, rows, width), BF16),) * 2,
        in_specs=[hbm] * 13,
        out_specs=(vmem, vmem),
        scratch_shapes=[
            pltpu.SMEM(ancestors.shape, jnp.int32),
            pltpu.SMEM(timestep.shape, jnp.int32),
            pltpu.VMEM(state.shape, BF16),
            pltpu.VMEM(state.shape, BF16),
            pltpu.VMEM(tables.shape, F32),
            pltpu.VMEM(perm.shape, BF16),
            pltpu.VMEM(w_in.shape, BF16),
            pltpu.VMEM(w_time.shape, BF16),
            pltpu.VMEM((ch, d), BF16),
            pltpu.VMEM((2, d, 3 * d), BF16),
            pltpu.VMEM((2, d, d), BF16),
            pltpu.VMEM((2, d, ff), BF16),
            pltpu.VMEM((2, ff, d), BF16),
            pltpu.VMEM((rows * (cols + 8), LANES), F32),
            pltpu.VMEM((rows * (cols + 8), LANES), F32),
            pltpu.VMEM((nrow, pair, rows, held, d), BF16),
            pltpu.VMEM((pair, nrow, rows, held, d), BF16),
            *[pltpu.VMEM((pair, nrow, rows, held, d), F32)] * 3,
            pltpu.VMEM((pair * height * held, LANES), F32),
            pltpu.VMEM((pair, height, flat), F32),
            pltpu.VMEM((ndom, nrow, rows, flat), BF16),
            pltpu.VMEM((teams, nrow, pair, rows, flat), BF16),
            pltpu.VMEM((pair, rows, width), BF16),
            pltpu.VMEM((teams, rows, width), BF16),
            pltpu.VMEM((teams, rows, width), BF16),
            dma((9,)),
            dma((2, 4)),
            dma,
            dma((pair,)),
            dma((pair,)),
            dma((teams,)),
            dma((teams,)),
            dma((steps, pair, nrow)),
            dma((steps, pair, nrow)),
            dma((halves, ndom, nrow)),
            dma((halves, ndom, nrow)),
        ],
        compiler_params=pltpu.CompilerParams(
            collective_id=0, has_side_effects=True, vmem_limit_bytes=56 * 1024 * 1024,
        ),
    )(
        ancestors, timestep, state, prev_pred, tables, perm, w_in, w_time,
        w_qkv, w_attn_out, w_up, w_down, w_out.T,
    )
    return pl.pallas_call(
        hand_out,
        out_shape=(whole, whole),
        in_specs=[vmem, vmem],
        out_specs=(hbm, hbm),
        scratch_shapes=[dma((2,))],
        compiler_params=pltpu.CompilerParams(vmem_limit_bytes=4 * 1024 * 1024),
    )(stepped, predicted)


def solution(mesh):
    part = P(("group", "dom"), "row", None)
    in_specs = (part, part, P("group"), P("group")) + (P(),) * 7
    return jax.shard_map(
        functools.partial(per_device, (mesh.shape["dom"], mesh.shape["row"])),
        mesh=mesh, in_specs=in_specs, out_specs=(part, part), check_vma=False,
    )
```

```python
import functools
import math

import jax
import jax.numpy as jnp
import numpy as np
from jax import lax
from jax.experimental import pallas as pl
from jax.experimental.pallas import tpu as pltpu
from jax.sharding import PartitionSpec as P

HEADS = 8
STEPS = 1000
STRIDE = 20
LANES = 128
MESH = pl.DeviceIdType.MESH
F32 = jnp.float32
BF16 = jnp.bfloat16


def unit(v):
    return lax.rsqrt(jnp.mean(v * v, axis=-1, keepdims=True) + 1e-06)


def rms(v):
    return v * unit(v)


def mm(a, b):
    return jnp.dot(a, b, preferred_element_type=F32)


def mm_nt(a, b):
    return lax.dot_general(a, b, (((1,), (1,)), ((), ())), preferred_element_type=F32)


def rope_tables(length, head, lanes):
    half = head // 2
    rates = np.exp(-math.log(10000.0) * np.arange(half) / half)
    angles = np.tile(np.arange(length)[:, None] * rates[None, :], (1, lanes // half))
    return np.cos(angles).astype(np.float32), np.sin(angles).astype(np.float32)


def halves_first(d, head):
    half = head // 2
    new = np.arange(d)
    old = (new % (d // 2)) // half * head + new // (d // 2) * half + new % half
    return (np.arange(d)[:, None] == old[None, :]).astype(np.float32)


def rotated(v, by, cos, sin, scale=1.0):
    a, c = v[:, : v.shape[1] // 2], v[:, v.shape[1] // 2 :]
    inv = lax.rsqrt(jnp.mean(v * v, axis=-1, keepdims=True) * (by * by) + 1e-06) * (by * scale)
    return jnp.concatenate([(a * cos - c * sin) * inv, (a * sin + c * cos) * inv], axis=1)


def attention(q, k, v, mask, head):
    n, d = q.shape
    lane = lax.broadcasted_iota(jnp.int32, (1, LANES), 1)
    wide_lane = lax.broadcasted_iota(jnp.int32, (1, d), 1) % (d // 2)
    per = LANES // head
    outs = []
    for part in range(len(v)):
        keys, vals = [], []
        for h in range(per):
            pick = jnp.where(lane // head == h, 1.0, 0.0).astype(BF16)
            pick_key = jnp.where(wide_lane // (head // 2) == part * per + h, 1.0, 0.0).astype(BF16)
            keys.append(k * pick_key)
            vals.append(
                jnp.concatenate([v[part] * pick, jnp.broadcast_to(pick, (n, LANES))], axis=1)
            )
        scores = mm_nt(q, jnp.concatenate(keys, axis=0))
        weights = jnp.exp2(scores.astype(BF16))
        if mask is not None:
            weights = weights * mask
        both = mm(weights, jnp.concatenate(vals, axis=0))
        outs.append(both[:, :LANES] / both[:, LANES:])
    return jnp.concatenate(outs, axis=1).astype(BF16)


def mlp(h, w_up, w_down):
    x = mm(rms(h).astype(BF16), w_up).astype(BF16)
    root = math.sqrt(2.0 / math.pi)
    inner = x * (root + (root * 0.044715) * (x * x))
    gated = x + x * jnp.tanh(inner)
    return (h + 0.5 * mm(gated, w_down)).astype(BF16)


def kernel(
    cfg,
    anc_hbm, time_hbm, state_hbm, prev_hbm, tab_hbm, perm_hbm, w_in_hbm, w_time_hbm,
    w_qkv_hbm, w_attn_hbm, w_up_hbm, w_down_hbm, w_out_hbm,
    state_out, pred_out,
    anc_ref, time_ref, state_ref, prev_ref, tab_ref, perm_ref, w_in_ref, w_time_ref, w_out_ref,
    w_qkv, w_attn, w_up, w_down,
    xs, xp, h1, hcol, q2, k2, v2, ptok, flats, sel, fin, spair, ssel, sfin,
    in_sem, w_sem, own_sem, sa_send, sa_recv, sb_send, sb_recv, h_send, h_recv, p_send, p_recv,
):
    ndom, nrow, rows, cols, ch, d, head, height, wide, flat, pair = cfg
    dom, row = lax.axis_index("dom"), lax.axis_index("row")
    mine = cols // nrow
    group = LANES // math.gcd(ch, LANES)
    glanes = group * ch
    held = mine // pair
    halves = held // wide
    scale = math.log2(math.e) / math.sqrt(head)
    teams = ndom // pair
    team, seat = lax.div(dom, pair), lax.rem(dom, pair)

    def fetch(i, src, dst):
        copy = pltpu.make_async_copy(src, dst, in_sem.at[i])
        copy.start()
        return copy

    got_state = [fetch(0, state_hbm, state_ref), fetch(1, prev_hbm, prev_ref)]
    got_time = [
        fetch(2, time_hbm, time_ref), fetch(3, tab_hbm, tab_ref), fetch(4, w_time_hbm, w_time_ref),
        fetch(5, w_in_hbm, w_in_ref), fetch(8, perm_hbm, perm_ref),
    ]

    pairs = ((w_qkv_hbm, w_qkv), (w_attn_hbm, w_attn), (w_up_hbm, w_up), (w_down_hbm, w_down))

    def load(b, i):
        src, dst = pairs[i]
        copy = pltpu.make_async_copy(src.at[b], dst.at[b], w_sem.at[b, i])
        copy.start()
        return copy

    got_time.append(load(0, 0))
    barrier = pltpu.get_barrier_semaphore()

    def greet(i, carry):
        pl.semaphore_signal(
            barrier,
            inc=1,
            device_id={"dom": lax.rem(dom + lax.div(i, nrow), ndom), "row": lax.rem(row + lax.rem(i, nrow), nrow)},
            device_id_type=MESH,
        )
        return carry

    lax.fori_loop(1, ndom * nrow, greet, 0, unroll=ndom * nrow <= 16)
    loads = [load(0, i) for i in range(1, 4)]
    got_late = [load(1, i) for i in range(4)]
    got_late += [fetch(6, anc_hbm, anc_ref), fetch(7, w_out_hbm, w_out_ref)]
    for copy in got_state + got_time:
        copy.wait()
    lot = state_ref.shape[2] // pair

    def mine_of(place):
        return state_ref.at[0, :, pl.ds(pl.multiple_of(place * lot, LANES), lot)]

    own = pltpu.make_async_copy(mine_of(seat), spair.at[seat], own_sem)
    own.start()

    pitch = xs.shape[0] // rows
    lane = lax.broadcasted_iota(jnp.int32, (rows, LANES), 1)

    def split(c, carry):
        base = pl.multiple_of(c * glanes, LANES)
        for ref, out in ((state_ref, xs), (prev_ref, xp)):
            tiles = [
                ref[0, :, pl.ds(pl.multiple_of(base + j * LANES, LANES), LANES)].astype(F32)
                for j in range(glanes // LANES)
            ]
            for t in range(group):
                j, off = divmod(t * ch, LANES)
                v = pltpu.roll(tiles[j], LANES - off, 1) if off else tiles[j]
                if off + ch > LANES:
                    v = jnp.where(lane < LANES - off, v, pltpu.roll(tiles[j + 1], LANES - off, 1))
                out[pl.ds(c * group + t, rows, stride=pitch), :] = v
        return carry

    lax.fori_loop(0, cols // group, split, 0, unroll=True)

    moment = time_ref[0].astype(F32)
    half = d // 2
    times = jnp.broadcast_to(moment, (1, LANES))
    now, nxt = level(times), level(times - STRIDE)
    c1, c2 = jnp.sqrt(now), jnp.sqrt(nxt)
    c3 = jnp.sqrt(1.0 - nxt) / jnp.sqrt(1.0 - now)
    angles = tab_ref[2 * cols + 16 * height :, :] * moment
    emb = jnp.concatenate([jnp.sin(angles), jnp.cos(angles)], axis=1)
    temb = jnp.dot(
        emb, w_time_ref[...].astype(F32),
        precision=lax.Precision.HIGHEST, preferred_element_type=F32,
    )[0:1]
    w_in = w_in_ref[...].astype(F32)
    gap = jnp.zeros((LANES - ch, d), F32)
    w_in = jnp.concatenate([w_in[:ch], gap, w_in[ch:], gap], axis=0).astype(BF16)

    def halve(b):
        for i in range(2):
            at = slice(i * d, (i + 1) * d)
            w_qkv[b, :, at] = mm(w_qkv[b, :, at], perm_ref[...]).astype(BF16)

    halve(0)
    for copy in loads:
        copy.wait()
    cos_r, sin_r = tab_ref[0:cols], tab_ref[cols : 2 * cols]
    step_rows = 2 if rows % 2 == 0 else 1

    others = [(e, k) for e in range(pair - 1, -1, -1) for k in range(nrow - 1, -1, -1) if (e, k) != (0, 0)]

    def h_copy(i, e, k):
        peer, place = lax.rem(row + k, nrow), lax.rem(seat + e, pair)
        span = pl.ds(i * step_rows, step_rows)
        return pltpu.make_async_remote_copy(
            src_ref=h1.at[peer, place, span],
            dst_ref=hcol.at[seat, row, span],
            send_sem=h_send.at[i, e, k],
            recv_sem=h_recv.at[i, e, k],
            device_id={"dom": team * pair + place, "row": peer},
            device_id_type=MESH,
        )

    def state_pair(e):
        return pltpu.make_async_remote_copy(
            src_ref=mine_of(lax.rem(seat + e, pair)),
            dst_ref=spair.at[seat],
            send_sem=sa_send.at[e],
            recv_sem=sa_recv.at[e],
            device_id={"dom": team * pair + lax.rem(seat + e, pair)},
            device_id_type=MESH,
        )

    def state_out_copy(e):
        there = lax.rem(dom + e, ndom)
        return pltpu.make_async_remote_copy(
            src_ref=ssel.at[there],
            dst_ref=sfin.at[team, seat],
            send_sem=sb_send.at[e],
            recv_sem=sb_recv.at[e],
            device_id={"dom": there},
            device_id_type=MESH,
        )

    upper = lax.div(dom, max(ndom // 2, 1))
    later = lax.div(upper + 1, 2)

    def far_first(j):
        return later * j + (1 - later) * (ndom - j)

    def pick(there):
        return jnp.clip(anc_ref[there] - team * pair, 0, pair - 1)

    def front(i):
        x = jnp.concatenate(
            [
                jnp.concatenate([v[r * pitch : r * pitch + cols, :].astype(BF16) for v in (xs, xp)], axis=1)
                for r in range(i * step_rows, (i + 1) * step_rows)
            ],
            axis=0,
        )
        h = mm(x, w_in) + temb
        low = h.astype(BF16)
        h = low.astype(F32)
        by = unit(h)
        qkv = mm(low, w_qkv[0])
        cos = jnp.concatenate([cos_r] * step_rows, axis=0)
        sin = jnp.concatenate([sin_r] * step_rows, axis=0)
        q = rotated(qkv[:, :d], by, cos, sin, scale).astype(BF16)
        k = rotated(qkv[:, d : 2 * d], by, cos, sin).astype(BF16)
        v = (qkv[:, 2 * d :] * by).astype(BF16)
        v = [v[:, p * LANES : (p + 1) * LANES] for p in range(d // LANES)]
        return h, q, k, v

    def middle(h, q, k, v):
        mixed = []
        for r in range(step_rows):
            a, b = r * cols, (r + 1) * cols
            mixed.append(attention(q[a:b], k[a:b], [x[a:b] for x in v], None, head))
        o = jnp.concatenate(mixed, axis=0)
        return (h + mm(o, w_attn[0])).astype(BF16).astype(F32)

    def back(i, h):
        h = mlp(h, w_up[0], w_down[0]).reshape(step_rows, cols, d)
        span = slice(i * step_rows, (i + 1) * step_rows)
        for g in range(nrow * pair):
            h1[g // pair, g % pair, span] = h[:, g * held : (g + 1) * held, :]

    def send(i):
        for e, k in others:
            h_copy(i, e, k).start()

    def enter():
        pl.semaphore_wait(barrier, ndom * nrow - 1)
        for e in range(1, pair):
            state_pair(e).start()

    made = front(0)
    enter()
    for i in range(rows // step_rows):
        h = middle(*made)
        if i + 1 < rows // step_rows:
            made = front(i + 1)
        back(i, h)
        send(i)

    for copy in got_late:
        copy.wait()

    hcol[seat, row] = h1[row, seat]
    halve(1)

    cos_c = tab_ref[2 * cols : 2 * cols + 8 * height].reshape(height, 8, LANES)
    sin_c = tab_ref[2 * cols + 8 * height : 2 * cols + 16 * height].reshape(height, 8, LANES)
    cos_c = jnp.concatenate([cos_c] * (held // 8), axis=1).reshape(nrow, rows, held, LANES)
    sin_c = jnp.concatenate([sin_c] * (held // 8), axis=1).reshape(nrow, rows, held, LANES)
    sub = height * wide
    n1 = pair * sub
    n2 = pair * nrow * step_rows * held
    per = LANES // head
    qi = lax.broadcasted_iota(jnp.int32, (sub, per * sub), 0)
    ki = lax.broadcasted_iota(jnp.int32, (sub, per * sub), 1)
    mask = jnp.where(qi % wide == ki % wide, 1.0, 0.0).astype(BF16)
    hlane = lax.broadcasted_iota(jnp.int32, (height // (2 if nrow % 2 == 0 else 1), LANES), 1)

    def project(i):
        span = slice(i * step_rows, (i + 1) * step_rows)
        low = hcol[:, :, span].reshape(n2, d)
        by = unit(low.astype(F32))
        qkv = mm(low, w_qkv[1])
        cos = jnp.concatenate([cos_c[:, span].reshape(n2 // pair, LANES)] * pair, axis=0)
        sin = jnp.concatenate([sin_c[:, span].reshape(n2 // pair, LANES)] * pair, axis=0)
        shape = (pair, nrow, step_rows, held, d)
        q2[:, :, span] = rotated(qkv[:, :d], by, cos, sin, scale).reshape(shape)
        k2[:, :, span] = rotated(qkv[:, d : 2 * d], by, cos, sin).reshape(shape)
        v2[:, :, span] = (qkv[:, 2 * d :] * by).reshape(shape)

    for i in range(rows // step_rows):
        for e, k in others:
            h_copy(i, e, k).wait_recv()
        if i == 0:
            own.wait()
            for e in range(1, pair):
                state_pair(e).wait_recv()
            for j in range(1, ndom):
                there = lax.rem(dom + far_first(j), ndom)
                ssel[there] = spair[pick(there)]
                state_out_copy(far_first(j)).start()
            sfin[team, seat] = spair[pick(dom)]
        project(i)

    def second(s):
        span = slice(s * wide, (s + 1) * wide)
        mixed = []
        for p in range(pair):
            q, k, v = (x[p, :, :, span, :].reshape(sub, d).astype(BF16) for x in (q2, k2, v2))
            v = [v[:, t * LANES : (t + 1) * LANES] for t in range(d // LANES)]
            mixed.append(attention(q, k, v, mask, head))
        o = jnp.concatenate(mixed, axis=0)
        h = hcol[...].astype(F32)[:, :, :, span, :].reshape(n1, d)
        return (h + mm(o, w_attn[1])).astype(BF16).astype(F32)

    cuts = 2 if nrow % 2 == 0 else 1
    part, peers = height // cuts, nrow // cuts
    ends = [0] + [(s + 1) * wide * ch // LANES for s in range(halves - 1)] + [flat // LANES]

    def shared(h, u):
        h = h.reshape(pair, height * wide, d)[:, u * part * wide : (u + 1) * part * wide]
        return h.reshape(pair * part * wide, d)

    def finish(s, u, low):
        out = mm_nt(low, w_out_ref[...]) * unit(low.astype(F32))

        def base(s, p):
            return s * n1 + (p * height + u * part) * wide

        for p in range(pair):
            ptok[base(s, p) : base(s, p) + part * wide, 0:ch] = out[p * part * wide : (p + 1) * part * wide]
        for p in range(pair):
            toks = {}
            for j in range(ends[s], ends[s + 1]):
                acc = None
                for t in range(j * LANES // ch, min((j * LANES + LANES - 1) // ch, (s + 1) * wide - 1) + 1):
                    if t not in toks:
                        toks[t] = ptok[pl.ds(base(t // wide, p) + t % wide, part, stride=wide), :]
                    at = t * ch - j * LANES
                    x = pltpu.roll(toks[t], at % LANES, 1) if at % LANES else toks[t]
                    acc = x if acc is None else jnp.where(hlane >= at, x, acc)
                flats[p, u * part : (u + 1) * part, j * LANES : (j + 1) * LANES] = acc
        span = slice(ends[s] * LANES, ends[s + 1] * LANES)
        for there in range(ndom):
            want = pick(there)
            for r in range(u * peers, (u + 1) * peers):
                sel[there, r, :, span] = flats[want, r * rows : (r + 1) * rows, span].astype(BF16)

    def p_copy(s, e, peer, sent, got):
        there = lax.rem(dom + e, ndom)
        span = pl.ds(ends[s] * LANES, (ends[s + 1] - ends[s]) * LANES)
        return pltpu.make_async_remote_copy(
            src_ref=sel.at[there, peer, :, span],
            dst_ref=fin.at[team, row, seat, :, span],
            send_sem=p_send.at[s, e, sent],
            recv_sem=p_recv.at[s, e, got],
            device_id={"dom": there, "row": peer},
            device_id_type=MESH,
        )

    def p_far(s, e, r):
        return p_copy(s, e, r, r, row)

    def p_near(s, k):
        return p_copy(s, 0, lax.rem(row + k, nrow), k, k)

    def p_all(s):
        return [p_copy(s, e, r, r, r) for e in range(1, ndom) for r in range(nrow)] + [
            p_near(s, k) for k in range(1, nrow)
        ]

    def post(s, u):
        for j in range(1, ndom):
            for r in range(u * peers, (u + 1) * peers):
                p_far(s, far_first(j), r).start()
        if u == cuts - 1:
            span = slice(ends[s] * LANES, ends[s + 1] * LANES)
            for k in range(1, nrow):
                p_near(s, k).start()
            fin[team, row, seat, :, span] = sel[dom, row, :, span]

    for s in range(halves):
        h = second(s)
        if s < halves - 1:
            low = mlp(h, w_up[1], w_down[1])
        for u in range(cuts):
            if s == halves - 1:
                finish(s, u, mlp(shared(h, u), w_up[1], w_down[1]))
            else:
                finish(s, u, shared(low, u))
            post(s, u)
    for e in range(1, ndom):
        state_out_copy(e).wait_recv()
    home = lax.div(anc_ref[dom], pair)

    for s in range(halves):
        for copy in p_all(s):
            copy.wait_recv()

    size = held * ch
    count = flat // LANES

    def piece(q, offset):
        tile, rem = divmod(offset, LANES)

        def load(j):
            x = fin[home, q // pair, q % pair, :, j * LANES : (j + 1) * LANES].astype(F32)
            return pltpu.roll(x, LANES - rem, 1) if rem else x

        low = load(tile) if tile >= 0 else None
        if not rem or tile + 1 >= count:
            return low
        high = load(tile + 1)
        return high if low is None else jnp.where(lane < LANES - rem, low, high)

    for j in range(cols * ch // LANES):
        start = j * LANES
        acc = None
        for q in range(start // size, (start + LANES - 1) // size + 1):
            x = piece(q, start - q * size)
            acc = x if acc is None else jnp.where(lane >= q * size - start, x, acc)
        acc = acc.astype(BF16)
        pred_out[0, :, start : start + LANES] = acc
        pred = acc.astype(F32)
        old = sfin[home, start // lot, :, start % lot : start % lot + LANES].astype(F32)
        state_out[0, :, start : start + LANES] = (c2 * pred + c3 * (old - c1 * pred)).astype(BF16)

    for e in range(1, pair):
        state_pair(e).wait_send()
    for e in range(1, ndom):
        state_out_copy(e).wait_send()
    for i in range(rows // step_rows):
        for e, k in others:
            h_copy(i, e, k).wait_send()
    for s in range(halves):
        for copy in p_all(s):
            copy.wait_send()


def level(moment):
    cosine = jnp.cos((moment / STEPS + 0.008) / 1.008 * math.pi / 2.0)
    return cosine * cosine


def hand_out(state_ref, pred_ref, new_state_ref, new_pred_ref, sems):
    first = pltpu.make_async_copy(state_ref, new_state_ref, sems.at[0])
    second = pltpu.make_async_copy(pred_ref, new_pred_ref, sems.at[1])
    first.start()
    second.start()
    first.wait()
    second.wait()


def per_device(
    sizes, state, prev_pred, ancestors, timestep, w_in, w_time, w_qkv, w_attn_out, w_up, w_down, w_out
):
    ndom, nrow = sizes
    _, rows, width = state.shape
    d, ch = w_out.shape
    cols, height, head = width // ch, rows * nrow, d // HEADS
    ff = w_up.shape[2]
    half = d // 2
    rates = np.exp(-math.log(10000.0) * np.arange(half) / half).astype(np.float32)
    cos_r, sin_r = rope_tables(cols, head, LANES)
    cos_c, sin_c = rope_tables(height, head, LANES)
    tables = jnp.asarray(
        np.concatenate(
            [
                cos_r, sin_r, np.repeat(cos_c, 8, axis=0), np.repeat(sin_c, 8, axis=0),
                np.tile(rates[None], (8, 1)),
            ]
        )
    )
    perm = jnp.asarray(halves_first(d, head).astype(jnp.bfloat16))
    mine = cols // nrow
    wide = min(8, mine)
    pair = max(p for p in range(1, ndom + 1) if ndom % p == 0 and p * p <= ndom and mine % (p * wide) == 0 and width % (p * LANES) == 0)
    teams, held = ndom // pair, mine // pair
    flat = -(-held * ch // LANES) * LANES
    halves, steps = held // wide, max(rows // 2, 1)
    cfg = (ndom, nrow, rows, cols, ch, d, head, height, wide, flat, pair)
    vmem = pl.BlockSpec(memory_space=pltpu.VMEM)
    hbm = pl.BlockSpec(memory_space=pl.ANY)
    whole = jax.ShapeDtypeStruct((1, rows, width), BF16)
    dma = pltpu.SemaphoreType.DMA
    stepped, predicted = pl.pallas_call(
        functools.partial(kernel, cfg),
        out_shape=(pltpu.VMEM((1, rows, width), BF16),) * 2,
        in_specs=[hbm] * 13,
        out_specs=(vmem, vmem),
        scratch_shapes=[
            pltpu.SMEM(ancestors.shape, jnp.int32),
            pltpu.SMEM(timestep.shape, jnp.int32),
            pltpu.VMEM(state.shape, BF16),
            pltpu.VMEM(state.shape, BF16),
            pltpu.VMEM(tables.shape, F32),
            pltpu.VMEM(perm.shape, BF16),
            pltpu.VMEM(w_in.shape, BF16),
            pltpu.VMEM(w_time.shape, BF16),
            pltpu.VMEM((ch, d), BF16),
            pltpu.VMEM((2, d, 3 * d), BF16),
            pltpu.VMEM((2, d, d), BF16),
            pltpu.VMEM((2, d, ff), BF16),
            pltpu.VMEM((2, ff, d), BF16),
            pltpu.VMEM((rows * (cols + 8), LANES), F32),
            pltpu.VMEM((rows * (cols + 8), LANES), F32),
            pltpu.VMEM((nrow, pair, rows, held, d), BF16),
            pltpu.VMEM((pair, nrow, rows, held, d), BF16),
            *[pltpu.VMEM((pair, nrow, rows, held, d), F32)] * 3,
            pltpu.VMEM((pair * height * held, LANES), F32),
            pltpu.VMEM((pair, height, flat), F32),
            pltpu.VMEM((ndom, nrow, rows, flat), BF16),
            pltpu.VMEM((teams, nrow, pair, rows, flat), BF16),
            pltpu.VMEM((pair, rows, width // pair), BF16),
            pltpu.VMEM((ndom, rows, width // pair), BF16),
            pltpu.VMEM((teams, pair, rows, width // pair), BF16),
            dma((9,)),
            dma((2, 4)),
            dma,
            dma((pair,)),
            dma((pair,)),
            dma((ndom,)),
            dma((ndom,)),
            dma((steps, pair, nrow)),
            dma((steps, pair, nrow)),
            dma((halves, ndom, nrow)),
            dma((halves, ndom, nrow)),
        ],
        compiler_params=pltpu.CompilerParams(
            collective_id=0, has_side_effects=True, vmem_limit_bytes=56 * 1024 * 1024,
        ),
    )(
        ancestors, timestep, state, prev_pred, tables, perm, w_in, w_time,
        w_qkv, w_attn_out, w_up, w_down, w_out.T,
    )
    return pl.pallas_call(
        hand_out,
        out_shape=(whole, whole),
        in_specs=[vmem, vmem],
        out_specs=(hbm, hbm),
        scratch_shapes=[dma((2,))],
        compiler_params=pltpu.CompilerParams(vmem_limit_bytes=4 * 1024 * 1024),
    )(stepped, predicted)


def solution(mesh):
    part = P(("group", "dom"), "row", None)
    in_specs = (part, part, P("group"), P("group")) + (P(),) * 7
    return jax.shard_map(
        functools.partial(per_device, (mesh.shape["dom"], mesh.shape["row"])),
        mesh=mesh, in_specs=in_specs, out_specs=(part, part), check_vma=False,
    )
```

```python
import functools
import math

import jax
import jax.numpy as jnp
import numpy as np
from jax import lax
from jax.experimental import pallas as pl
from jax.experimental.pallas import tpu as pltpu
from jax.sharding import PartitionSpec as P

HEADS = 8
STEPS = 1000
STRIDE = 20
LANES = 128
MESH = pl.DeviceIdType.MESH
F32 = jnp.float32
BF16 = jnp.bfloat16


def unit(v):
    return lax.rsqrt(jnp.mean(v * v, axis=-1, keepdims=True) + 1e-06)


def rms(v):
    return v * unit(v)


def mm(a, b):
    return jnp.dot(a, b, preferred_element_type=F32)


def mm_nt(a, b):
    return lax.dot_general(a, b, (((1,), (1,)), ((), ())), preferred_element_type=F32)


def rope_tables(length, head, lanes):
    half = head // 2
    rates = np.exp(-math.log(10000.0) * np.arange(half) / half)
    angles = np.tile(np.arange(length)[:, None] * rates[None, :], (1, lanes // half))
    return np.cos(angles).astype(np.float32), np.sin(angles).astype(np.float32)


def halves_first(d, head):
    half = head // 2
    new = np.arange(d)
    old = (new % (d // 2)) // half * head + new // (d // 2) * half + new % half
    return (np.arange(d)[:, None] == old[None, :]).astype(np.float32)


def rotated(v, by, cos, sin, scale=1.0):
    a, c = v[:, : v.shape[1] // 2], v[:, v.shape[1] // 2 :]
    inv = lax.rsqrt(jnp.mean(v * v, axis=-1, keepdims=True) * (by * by) + 1e-06) * (by * scale)
    return jnp.concatenate([(a * cos - c * sin) * inv, (a * sin + c * cos) * inv], axis=1)


def attention(q, k, v, mask, head):
    n, d = q.shape
    lane = lax.broadcasted_iota(jnp.int32, (1, LANES), 1)
    wide_lane = lax.broadcasted_iota(jnp.int32, (1, d), 1) % (d // 2)
    per = LANES // head
    outs = []
    for part in range(len(v)):
        keys, vals = [], []
        for h in range(per):
            pick = jnp.where(lane // head == h, 1.0, 0.0).astype(BF16)
            pick_key = jnp.where(wide_lane // (head // 2) == part * per + h, 1.0, 0.0).astype(BF16)
            keys.append(k * pick_key)
            vals.append(
                jnp.concatenate([v[part] * pick, jnp.broadcast_to(pick, (n, LANES))], axis=1)
            )
        scores = mm_nt(q, jnp.concatenate(keys, axis=0))
        weights = jnp.exp2(scores.astype(BF16))
        if mask is not None:
            weights = weights * mask
        both = mm(weights, jnp.concatenate(vals, axis=0))
        outs.append(both[:, :LANES] / both[:, LANES:])
    return jnp.concatenate(outs, axis=1).astype(BF16)


def mlp(h, w_up, w_down):
    x = mm(rms(h).astype(BF16), w_up).astype(BF16)
    root = math.sqrt(2.0 / math.pi)
    inner = x * (root + (root * 0.044715) * (x * x))
    gated = x + x * jnp.tanh(inner)
    return (h + 0.5 * mm(gated, w_down)).astype(BF16)


def kernel(
    cfg,
    anc_hbm, time_hbm, state_hbm, prev_hbm, tab_hbm, perm_hbm, w_in_hbm, w_time_hbm,
    w_qkv_hbm, w_attn_hbm, w_up_hbm, w_down_hbm, w_out_hbm,
    state_out, pred_out,
    anc_ref, time_ref, state_ref, prev_ref, tab_ref, perm_ref, w_in_ref, w_time_ref, w_out_ref,
    w_qkv, w_attn, w_up, w_down,
    xs, xp, h1, hcol, q2, k2, v2, ptok, flats, sel, fin, spair, ssel, sfin,
    in_sem, w_sem, own_sem, sa_send, sa_recv, sb_send, sb_recv, h_send, h_recv, p_send, p_recv,
):
    ndom, nrow, rows, cols, ch, d, head, height, wide, flat, pair = cfg
    dom, row = lax.axis_index("dom"), lax.axis_index("row")
    mine = cols // nrow
    group = LANES // math.gcd(ch, LANES)
    glanes = group * ch
    held = mine // pair
    halves = held // wide
    scale = math.log2(math.e) / math.sqrt(head)
    teams = ndom // pair
    team, seat = lax.div(dom, pair), lax.rem(dom, pair)

    def fetch(i, src, dst):
        copy = pltpu.make_async_copy(src, dst, in_sem.at[i])
        copy.start()
        return copy

    got_state = [fetch(0, state_hbm, state_ref), fetch(1, prev_hbm, prev_ref)]
    got_time = [
        fetch(2, time_hbm, time_ref), fetch(3, tab_hbm, tab_ref), fetch(4, w_time_hbm, w_time_ref),
        fetch(5, w_in_hbm, w_in_ref), fetch(8, perm_hbm, perm_ref),
    ]

    pairs = ((w_qkv_hbm, w_qkv), (w_attn_hbm, w_attn), (w_up_hbm, w_up), (w_down_hbm, w_down))

    def load(b, i):
        src, dst = pairs[i]
        copy = pltpu.make_async_copy(src.at[b], dst.at[b], w_sem.at[b, i])
        copy.start()
        return copy

    got_time.append(load(0, 0))
    barrier = pltpu.get_barrier_semaphore()

    def greet(i, carry):
        pl.semaphore_signal(
            barrier,
            inc=1,
            device_id={"dom": lax.rem(dom + lax.div(i, nrow), ndom), "row": lax.rem(row + lax.rem(i, nrow), nrow)},
            device_id_type=MESH,
        )
        return carry

    lax.fori_loop(1, ndom * nrow, greet, 0, unroll=ndom * nrow <= 16)
    loads = [load(0, i) for i in range(1, 4)]
    got_late = [load(1, i) for i in range(4)]
    got_late += [fetch(6, anc_hbm, anc_ref), fetch(7, w_out_hbm, w_out_ref)]
    for copy in got_state + got_time:
        copy.wait()
    lot = state_ref.shape[2] // pair

    def mine_of(place):
        return state_ref.at[0, :, pl.ds(pl.multiple_of(place * lot, LANES), lot)]

    own = pltpu.make_async_copy(mine_of(seat), spair.at[seat], own_sem)
    own.start()

    pitch = xs.shape[0] // rows
    lane = lax.broadcasted_iota(jnp.int32, (rows, LANES), 1)

    def split(c, carry):
        base = pl.multiple_of(c * glanes, LANES)
        for ref, out in ((state_ref, xs), (prev_ref, xp)):
            tiles = [
                ref[0, :, pl.ds(pl.multiple_of(base + j * LANES, LANES), LANES)].astype(F32)
                for j in range(glanes // LANES)
            ]
            for t in range(group):
                j, off = divmod(t * ch, LANES)
                v = pltpu.roll(tiles[j], LANES - off, 1) if off else tiles[j]
                if off + ch > LANES:
                    v = jnp.where(lane < LANES - off, v, pltpu.roll(tiles[j + 1], LANES - off, 1))
                out[pl.ds(c * group + t, rows, stride=pitch), :] = v
        return carry

    lax.fori_loop(0, cols // group, split, 0, unroll=True)

    moment = time_ref[0].astype(F32)
    half = d // 2
    times = jnp.broadcast_to(moment, (1, LANES))
    now, nxt = level(times), level(times - STRIDE)
    c1, c2 = jnp.sqrt(now), jnp.sqrt(nxt)
    c3 = jnp.sqrt(1.0 - nxt) / jnp.sqrt(1.0 - now)
    angles = tab_ref[2 * cols + 16 * height :, :] * moment
    emb = jnp.concatenate([jnp.sin(angles), jnp.cos(angles)], axis=1)
    temb = jnp.dot(
        emb, w_time_ref[...].astype(F32),
        precision=lax.Precision.HIGHEST, preferred_element_type=F32,
    )[0:1]
    w_in = w_in_ref[...].astype(F32)
    gap = jnp.zeros((LANES - ch, d), F32)
    w_in = jnp.concatenate([w_in[:ch], gap, w_in[ch:], gap], axis=0).astype(BF16)

    def halve(b):
        for i in range(2):
            at = slice(i * d, (i + 1) * d)
            w_qkv[b, :, at] = mm(w_qkv[b, :, at], perm_ref[...]).astype(BF16)

    halve(0)
    for copy in loads:
        copy.wait()
    cos_r, sin_r = tab_ref[0:cols], tab_ref[cols : 2 * cols]
    step_rows = 2 if rows % 2 == 0 else 1

    others = [(e, k) for k in range(nrow - 1, -1, -1) for e in range(pair - 1, -1, -1) if (e, k) != (0, 0)]

    def h_copy(i, e, k):
        peer, place = lax.rem(row + k, nrow), lax.rem(seat + e, pair)
        span = pl.ds(i * step_rows, step_rows)
        return pltpu.make_async_remote_copy(
            src_ref=h1.at[peer, place, span],
            dst_ref=hcol.at[seat, row, span],
            send_sem=h_send.at[i, e, k],
            recv_sem=h_recv.at[i, e, k],
            device_id={"dom": team * pair + place, "row": peer},
            device_id_type=MESH,
        )

    def state_pair(e):
        return pltpu.make_async_remote_copy(
            src_ref=mine_of(lax.rem(seat + e, pair)),
            dst_ref=spair.at[seat],
            send_sem=sa_send.at[e],
            recv_sem=sa_recv.at[e],
            device_id={"dom": team * pair + lax.rem(seat + e, pair)},
            device_id_type=MESH,
        )

    def state_out_copy(e):
        there = lax.rem(dom + e, ndom)
        return pltpu.make_async_remote_copy(
            src_ref=ssel.at[there],
            dst_ref=sfin.at[team, seat],
            send_sem=sb_send.at[e],
            recv_sem=sb_recv.at[e],
            device_id={"dom": there},
            device_id_type=MESH,
        )

    upper = lax.div(dom, max(ndom // 2, 1))
    later = lax.div(upper + 1, 2)

    def far_first(j):
        return later * j + (1 - later) * (ndom - j)

    def pick(there):
        return jnp.clip(anc_ref[there] - team * pair, 0, pair - 1)

    def front(i):
        x = jnp.concatenate(
            [
                jnp.concatenate([v[r * pitch : r * pitch + cols, :].astype(BF16) for v in (xs, xp)], axis=1)
                for r in range(i * step_rows, (i + 1) * step_rows)
            ],
            axis=0,
        )
        h = mm(x, w_in) + temb
        low = h.astype(BF16)
        h = low.astype(F32)
        by = unit(h)
        qkv = mm(low, w_qkv[0])
        cos = jnp.concatenate([cos_r] * step_rows, axis=0)
        sin = jnp.concatenate([sin_r] * step_rows, axis=0)
        q = rotated(qkv[:, :d], by, cos, sin, scale).astype(BF16)
        k = rotated(qkv[:, d : 2 * d], by, cos, sin).astype(BF16)
        v = (qkv[:, 2 * d :] * by).astype(BF16)
        v = [v[:, p * LANES : (p + 1) * LANES] for p in range(d // LANES)]
        return h, q, k, v

    def middle(h, q, k, v):
        mixed = []
        for r in range(step_rows):
            a, b = r * cols, (r + 1) * cols
            mixed.append(attention(q[a:b], k[a:b], [x[a:b] for x in v], None, head))
        o = jnp.concatenate(mixed, axis=0)
        return (h + mm(o, w_attn[0])).astype(BF16).astype(F32)

    def back(i, h):
        h = mlp(h, w_up[0], w_down[0]).reshape(step_rows, cols, d)
        span = slice(i * step_rows, (i + 1) * step_rows)
        for g in range(nrow * pair):
            h1[g // pair, g % pair, span] = h[:, g * held : (g + 1) * held, :]

    def send(i):
        for e, k in others:
            h_copy(i, e, k).start()

    def enter():
        pl.semaphore_wait(barrier, ndom * nrow - 1)
        for e in range(1, pair):
            state_pair(e).start()

    made = front(0)
    enter()
    for i in range(rows // step_rows):
        h = middle(*made)
        if i + 1 < rows // step_rows:
            made = front(i + 1)
        back(i, h)
        send(i)

    for copy in got_late:
        copy.wait()

    hcol[seat, row] = h1[row, seat]
    halve(1)

    cos_c = tab_ref[2 * cols : 2 * cols + 8 * height].reshape(height, 8, LANES)
    sin_c = tab_ref[2 * cols + 8 * height : 2 * cols + 16 * height].reshape(height, 8, LANES)
    cos_c = jnp.concatenate([cos_c] * (held // 8), axis=1).reshape(nrow, rows, held, LANES)
    sin_c = jnp.concatenate([sin_c] * (held // 8), axis=1).reshape(nrow, rows, held, LANES)
    sub = height * wide
    n1 = pair * sub
    n2 = pair * nrow * step_rows * held
    per = LANES // head
    qi = lax.broadcasted_iota(jnp.int32, (sub, per * sub), 0)
    ki = lax.broadcasted_iota(jnp.int32, (sub, per * sub), 1)
    mask = jnp.where(qi % wide == ki % wide, 1.0, 0.0).astype(BF16)
    hlane = lax.broadcasted_iota(jnp.int32, (height // (2 if nrow % 2 == 0 else 1), LANES), 1)

    def project(i):
        span = slice(i * step_rows, (i + 1) * step_rows)
        low = hcol[:, :, span].reshape(n2, d)
        by = unit(low.astype(F32))
        qkv = mm(low, w_qkv[1])
        cos = jnp.concatenate([cos_c[:, span].reshape(n2 // pair, LANES)] * pair, axis=0)
        sin = jnp.concatenate([sin_c[:, span].reshape(n2 // pair, LANES)] * pair, axis=0)
        shape = (pair, nrow, step_rows, held, d)
        q2[:, :, span] = rotated(qkv[:, :d], by, cos, sin, scale).reshape(shape)
        k2[:, :, span] = rotated(qkv[:, d : 2 * d], by, cos, sin).reshape(shape)
        v2[:, :, span] = (qkv[:, 2 * d :] * by).reshape(shape)

    for i in range(rows // step_rows):
        for e, k in others:
            h_copy(i, e, k).wait_recv()
        if i == 0:
            own.wait()
            for e in range(1, pair):
                state_pair(e).wait_recv()
            for j in range(1, ndom):
                there = lax.rem(dom + far_first(j), ndom)
                ssel[there] = spair[pick(there)]
                state_out_copy(far_first(j)).start()
            sfin[team, seat] = spair[pick(dom)]
        project(i)

    def second(s):
        span = slice(s * wide, (s + 1) * wide)
        mixed = []
        for p in range(pair):
            q, k, v = (x[p, :, :, span, :].reshape(sub, d).astype(BF16) for x in (q2, k2, v2))
            v = [v[:, t * LANES : (t + 1) * LANES] for t in range(d // LANES)]
            mixed.append(attention(q, k, v, mask, head))
        o = jnp.concatenate(mixed, axis=0)
        h = hcol[...].astype(F32)[:, :, :, span, :].reshape(n1, d)
        return (h + mm(o, w_attn[1])).astype(BF16).astype(F32)

    cuts = 2 if nrow % 2 == 0 else 1
    part, peers = height // cuts, nrow // cuts
    ends = [0] + [(s + 1) * wide * ch // LANES for s in range(halves - 1)] + [flat // LANES]

    def shared(h, u):
        h = h.reshape(pair, height * wide, d)[:, u * part * wide : (u + 1) * part * wide]
        return h.reshape(pair * part * wide, d)

    def finish(s, u, low):
        out = mm_nt(low, w_out_ref[...]) * unit(low.astype(F32))

        def base(s, p):
            return s * n1 + (p * height + u * part) * wide

        for p in range(pair):
            ptok[base(s, p) : base(s, p) + part * wide, 0:ch] = out[p * part * wide : (p + 1) * part * wide]
        for p in range(pair):
            toks = {}
            for j in range(ends[s], ends[s + 1]):
                acc = None
                for t in range(j * LANES // ch, min((j * LANES + LANES - 1) // ch, (s + 1) * wide - 1) + 1):
                    if t not in toks:
                        toks[t] = ptok[pl.ds(base(t // wide, p) + t % wide, part, stride=wide), :]
                    at = t * ch - j * LANES
                    x = pltpu.roll(toks[t], at % LANES, 1) if at % LANES else toks[t]
                    acc = x if acc is None else jnp.where(hlane >= at, x, acc)
                flats[p, u * part : (u + 1) * part, j * LANES : (j + 1) * LANES] = acc
        span = slice(ends[s] * LANES, ends[s + 1] * LANES)
        for there in range(ndom):
            want = pick(there)
            for r in range(u * peers, (u + 1) * peers):
                sel[there, r, :, span] = flats[want, r * rows : (r + 1) * rows, span].astype(BF16)

    def p_copy(s, e, peer, sent, got):
        there = lax.rem(dom + e, ndom)
        span = pl.ds(ends[s] * LANES, (ends[s + 1] - ends[s]) * LANES)
        return pltpu.make_async_remote_copy(
            src_ref=sel.at[there, peer, :, span],
            dst_ref=fin.at[team, row, seat, :, span],
            send_sem=p_send.at[s, e, sent],
            recv_sem=p_recv.at[s, e, got],
            device_id={"dom": there, "row": peer},
            device_id_type=MESH,
        )

    def p_far(s, e, r):
        return p_copy(s, e, r, r, row)

    def p_near(s, k):
        return p_copy(s, 0, lax.rem(row + k, nrow), k, k)

    def p_all(s):
        return [p_copy(s, e, r, r, r) for e in range(1, ndom) for r in range(nrow)] + [
            p_near(s, k) for k in range(1, nrow)
        ]

    def post(s, u):
        for j in range(1, ndom):
            for r in range(u * peers, (u + 1) * peers):
                p_far(s, far_first(j), r).start()
        if u == cuts - 1:
            span = slice(ends[s] * LANES, ends[s + 1] * LANES)
            for k in range(1, nrow):
                p_near(s, k).start()
            fin[team, row, seat, :, span] = sel[dom, row, :, span]

    for s in range(halves):
        h = second(s)
        if s < halves - 1:
            low = mlp(h, w_up[1], w_down[1])
        for u in range(cuts):
            if s == halves - 1:
                finish(s, u, mlp(shared(h, u), w_up[1], w_down[1]))
            else:
                finish(s, u, shared(low, u))
            post(s, u)
    for e in range(1, ndom):
        state_out_copy(e).wait_recv()
    home = lax.div(anc_ref[dom], pair)

    for s in range(halves):
        for copy in p_all(s):
            copy.wait_recv()

    size = held * ch
    count = flat // LANES

    def piece(q, offset):
        tile, rem = divmod(offset, LANES)

        def load(j):
            x = fin[home, q // pair, q % pair, :, j * LANES : (j + 1) * LANES].astype(F32)
            return pltpu.roll(x, LANES - rem, 1) if rem else x

        low = load(tile) if tile >= 0 else None
        if not rem or tile + 1 >= count:
            return low
        high = load(tile + 1)
        return high if low is None else jnp.where(lane < LANES - rem, low, high)

    for j in range(cols * ch // LANES):
        start = j * LANES
        acc = None
        for q in range(start // size, (start + LANES - 1) // size + 1):
            x = piece(q, start - q * size)
            acc = x if acc is None else jnp.where(lane >= q * size - start, x, acc)
        acc = acc.astype(BF16)
        pred_out[0, :, start : start + LANES] = acc
        pred = acc.astype(F32)
        old = sfin[home, start // lot, :, start % lot : start % lot + LANES].astype(F32)
        state_out[0, :, start : start + LANES] = (c2 * pred + c3 * (old - c1 * pred)).astype(BF16)

    for e in range(1, pair):
        state_pair(e).wait_send()
    for e in range(1, ndom):
        state_out_copy(e).wait_send()
    for i in range(rows // step_rows):
        for e, k in others:
            h_copy(i, e, k).wait_send()
    for s in range(halves):
        for copy in p_all(s):
            copy.wait_send()


def level(moment):
    cosine = jnp.cos((moment / STEPS + 0.008) / 1.008 * math.pi / 2.0)
    return cosine * cosine


def hand_out(state_ref, pred_ref, new_state_ref, new_pred_ref, sems):
    first = pltpu.make_async_copy(state_ref, new_state_ref, sems.at[0])
    second = pltpu.make_async_copy(pred_ref, new_pred_ref, sems.at[1])
    first.start()
    second.start()
    first.wait()
    second.wait()


def per_device(
    sizes, state, prev_pred, ancestors, timestep, w_in, w_time, w_qkv, w_attn_out, w_up, w_down, w_out
):
    ndom, nrow = sizes
    _, rows, width = state.shape
    d, ch = w_out.shape
    cols, height, head = width // ch, rows * nrow, d // HEADS
    ff = w_up.shape[2]
    half = d // 2
    rates = np.exp(-math.log(10000.0) * np.arange(half) / half).astype(np.float32)
    cos_r, sin_r = rope_tables(cols, head, LANES)
    cos_c, sin_c = rope_tables(height, head, LANES)
    tables = jnp.asarray(
        np.concatenate(
            [
                cos_r, sin_r, np.repeat(cos_c, 8, axis=0), np.repeat(sin_c, 8, axis=0),
                np.tile(rates[None], (8, 1)),
            ]
        )
    )
    perm = jnp.asarray(halves_first(d, head).astype(jnp.bfloat16))
    mine = cols // nrow
    wide = min(8, mine)
    pair = max(p for p in range(1, ndom + 1) if ndom % p == 0 and p * p <= ndom and mine % (p * wide) == 0 and width % (p * LANES) == 0)
    teams, held = ndom // pair, mine // pair
    flat = -(-held * ch // LANES) * LANES
    halves, steps = held // wide, max(rows // 2, 1)
    cfg = (ndom, nrow, rows, cols, ch, d, head, height, wide, flat, pair)
    vmem = pl.BlockSpec(memory_space=pltpu.VMEM)
    hbm = pl.BlockSpec(memory_space=pl.ANY)
    whole = jax.ShapeDtypeStruct((1, rows, width), BF16)
    dma = pltpu.SemaphoreType.DMA
    stepped, predicted = pl.pallas_call(
        functools.partial(kernel, cfg),
        out_shape=(pltpu.VMEM((1, rows, width), BF16),) * 2,
        in_specs=[hbm] * 13,
        out_specs=(vmem, vmem),
        scratch_shapes=[
            pltpu.SMEM(ancestors.shape, jnp.int32),
            pltpu.SMEM(timestep.shape, jnp.int32),
            pltpu.VMEM(state.shape, BF16),
            pltpu.VMEM(state.shape, BF16),
            pltpu.VMEM(tables.shape, F32),
            pltpu.VMEM(perm.shape, BF16),
            pltpu.VMEM(w_in.shape, BF16),
            pltpu.VMEM(w_time.shape, BF16),
            pltpu.VMEM((ch, d), BF16),
            pltpu.VMEM((2, d, 3 * d), BF16),
            pltpu.VMEM((2, d, d), BF16),
            pltpu.VMEM((2, d, ff), BF16),
            pltpu.VMEM((2, ff, d), BF16),
            pltpu.VMEM((rows * (cols + 8), LANES), F32),
            pltpu.VMEM((rows * (cols + 8), LANES), F32),
            pltpu.VMEM((nrow, pair, rows, held, d), BF16),
            pltpu.VMEM((pair, nrow, rows, held, d), BF16),
            *[pltpu.VMEM((pair, nrow, rows, held, d), F32)] * 3,
            pltpu.VMEM((pair * height * held, LANES), F32),
            pltpu.VMEM((pair, height, flat), F32),
            pltpu.VMEM((ndom, nrow, rows, flat), BF16),
            pltpu.VMEM((teams, nrow, pair, rows, flat), BF16),
            pltpu.VMEM((pair, rows, width // pair), BF16),
            pltpu.VMEM((ndom, rows, width // pair), BF16),
            pltpu.VMEM((teams, pair, rows, width // pair), BF16),
            dma((9,)),
            dma((2, 4)),
            dma,
            dma((pair,)),
            dma((pair,)),
            dma((ndom,)),
            dma((ndom,)),
            dma((steps, pair, nrow)),
            dma((steps, pair, nrow)),
            dma((halves, ndom, nrow)),
            dma((halves, ndom, nrow)),
        ],
        compiler_params=pltpu.CompilerParams(
            collective_id=0, has_side_effects=True, vmem_limit_bytes=56 * 1024 * 1024,
        ),
    )(
        ancestors, timestep, state, prev_pred, tables, perm, w_in, w_time,
        w_qkv, w_attn_out, w_up, w_down, w_out.T,
    )
    return pl.pallas_call(
        hand_out,
        out_shape=(whole, whole),
        in_specs=[vmem, vmem],
        out_specs=(hbm, hbm),
        scratch_shapes=[dma((2,))],
        compiler_params=pltpu.CompilerParams(vmem_limit_bytes=4 * 1024 * 1024),
    )(stepped, predicted)


def solution(mesh):
    part = P(("group", "dom"), "row", None)
    in_specs = (part, part, P("group"), P("group")) + (P(),) * 7
    return jax.shard_map(
        functools.partial(per_device, (mesh.shape["dom"], mesh.shape["row"])),
        mesh=mesh, in_specs=in_specs, out_specs=(part, part), check_vma=False,
    )
```
